512 devices in a mesh: depth: 32 (over x, y, core), height: 16 (over z).
Axes of the slice: x: 4, y: 4, z: 16, core: 2. Of those that a mesh axis runs over, the one named last changes fastest.
Arguments:
- middle_input: bfloat16 [64, 32, 64, 128], P('depth', None, 'height'), may hold values from -6 to 6
- middle_cotangent: bfloat16 [64, 32, 64, 128], P('depth', None, 'height'), may hold values from -6 to 6
- middle_weight: bfloat16 [3, 3, 3, 32, 32], replicated, may hold values from -0.21875 to 0.21875
- coarse_input: bfloat16 [32, 32, 64, 128], P('depth', 'height'), may hold values from -6 to 6
- coarse_cotangent: bfloat16 [32, 32, 64, 128], P('depth', 'height'), may hold values from -6 to 6
- coarse_weight: bfloat16 [3, 3, 3, 128, 128], P(None, None, None, None, 'depth'), may hold values from -0.109375 to 0.109375
Outputs:
- middle_output: bfloat16 [64, 32, 64, 128], P('depth', None, 'height')
- middle_input_grad: bfloat16 [64, 32, 64, 128], P('depth', None, 'height')
- middle_weight_grad: float32 [3, 3, 3, 32, 32], replicated
- coarse_output: bfloat16 [32, 32, 64, 128], P('depth', 'height')
- coarse_input_grad: bfloat16 [32, 32, 64, 128], P('depth', 'height')
- coarse_weight_grad: float32 [3, 3, 3, 128, 128], P(None, None, None, None, 'depth')
The draws below stay inside these ranges and needn't reach their ends.
All inputs are finite; a program needn't handle non-finite values.
Results may differ from the reference program's by a relative error of at most 0.001.
Values may be sent and summed in bfloat16 or wider, within the bound.
A program may use at most 64 MiB of HBM per device.

```python
import math
import jax
import jax.numpy as jnp
from jax import lax

CH2 = 32
CH3 = 128
WID3 = 64
ND3 = 32
NH3 = 32
ND2 = 64
NH2 = 64
WID2 = 128
VOX2 = 524288
VOX3 = 65536


def raised(entries, key, source, target, shards_of, factor):
    def block_of(dim):
        return (jnp.arange(entries.shape[dim]) // (entries.shape[dim] // shards_of)).reshape((-1,) + (1,) * (entries.ndim - 1 - dim))

    one_side = jax.random.permutation(key, shards_of)[block_of(target)]
    far = (block_of(target) + shards_of // 2) % shards_of
    return jnp.where((block_of(source) == one_side) | (block_of(source) == far), factor * entries, entries)


def block_scale(stream_key, extent, split, least, largest):
    def one(dim, blocks):
        steps = jax.random.uniform(jax.random.fold_in(jax.random.fold_in(stream_key, 6), dim), (blocks,), jnp.float32, least / len(split), largest / len(split))
        return jnp.repeat(jnp.exp(steps), extent[dim] // blocks).reshape((-1,) + (1,) * (len(extent) - dim - 1))

    level = one(*split[0])
    for cut in split[1:]:
        level = level * one(*cut)
    return level


def centred(own_key, extent, deviation, bound, cuts=(), dtype=jnp.bfloat16):
    entries = deviation * jax.random.normal(own_key, extent, jnp.float32)
    if cuts:
        entries = entries * block_scale(own_key, extent, cuts, -0.22, 0.18)
    return jnp.clip(entries, -bound, bound).astype(dtype)


def bell_draw_with(rng, shape, width, most, pieces, heavy, dtype=jnp.bfloat16):
    values = width * jax.random.normal(rng, shape, jnp.float32)
    if pieces:
        values = values * block_scale(rng, shape, pieces, -0.22, 0.18)
    return jnp.clip(raised(values, jax.random.fold_in(rng, 3), *heavy), -most, most).astype(dtype)


def setup_inputs(seed: int = 0) -> dict:
    arg_keys = jax.random.split(jax.random.key(seed), 7)
    return {
        "middle_input": centred(arg_keys[0], (ND2, CH2, NH2, WID2), 1.0, 6.0, ((0, 32), (2, 16))),
        "middle_cotangent": centred(arg_keys[1], (ND2, CH2, NH2, WID2), 1.0, 6.0, ((0, 32), (2, 16))),
        "middle_weight": centred(arg_keys[2], (3, 3, 3, CH2, CH2), (27 * CH2) ** -0.5, 0.21875),
        "coarse_input": centred(arg_keys[3], (ND3, NH3, WID3, CH3), 1.0, 6.0, ((0, 32), (1, 16))),
        "coarse_cotangent": bell_draw_with(arg_keys[4], (ND3, NH3, WID3, CH3), 1.0, 6.0, ((0, 32), (1, 16)), (0, 3, 32, 2.75)),
        "coarse_weight": centred(arg_keys[5], (3, 3, 3, CH3, CH3), (27 * CH3) ** -0.5, 0.109375, ((4, 32),)),
    }


def convolve(volume, weight, layout):
    return lax.conv_general_dilated(volume, weight, (1, 1, 1), ((1, 1), (1, 1), (1, 1)), dimension_numbers=(layout, 'DHWIO', layout), precision=lax.Precision.HIGHEST)

def run_level(source, upstream, weight, layout, voxels):
    weight32 = weight.astype(jnp.float32)

    def forward(volume, kernel):
        return convolve(volume, kernel, layout)
    output, pullback = jax.vjp(forward, source, weight32)
    grad_in, grad_weight = pullback(upstream)
    factor = 1.0 / math.sqrt(voxels)
    return (output, grad_in, grad_weight * factor)

def second_level(volume, cotangent, weight, voxels):
    source = jnp.transpose(volume.astype(jnp.float32), (1, 0, 2, 3))[None]
    upstream = jnp.transpose(cotangent.astype(jnp.float32), (1, 0, 2, 3))[None]
    output, grad_in, grad_weight = run_level(source, upstream, weight, 'NCDHW', voxels)
    output = jnp.transpose(output[0], (1, 0, 2, 3)).astype(jnp.bfloat16)
    grad_in = jnp.transpose(grad_in[0], (1, 0, 2, 3)).astype(jnp.bfloat16)
    return (output, grad_in, grad_weight)

def reference(middle_input, middle_cotangent, middle_weight, coarse_input, coarse_cotangent, coarse_weight):
    middle_out, middle_dx, middle_dw = second_level(middle_input, middle_cotangent, middle_weight, VOX2)
    source = coarse_input.astype(jnp.float32)[None]
    upstream = coarse_cotangent.astype(jnp.float32)[None]
    coarse_out, coarse_dx, coarse_dw = run_level(source, upstream, coarse_weight, 'NDHWC', VOX3)
    return (middle_out, middle_dx, middle_dw, coarse_out[0].astype(jnp.bfloat16), coarse_dx[0].astype(jnp.bfloat16), coarse_dw)
```

```python
import math

import jax
import jax.numpy as jnp
from jax import lax
from jax.sharding import Mesh
from jax.sharding import PartitionSpec as P

DEPTH = ("depth_0", "depth_1", "depth_2")


def padded_2(x, sides, width):
    for axis, dim in sides:
        peers, length = (lax.axis_size(axis), x.shape[dim])
        up = [(i, (i + 1) % peers) for i in range(peers - 1)]
        down = [(j, i) for i, j in up]
        last = lax.slice_in_dim(x, length - width, length, axis=dim)
        leading = lax.slice_in_dim(x, 0, width, axis=dim)
        before = lax.ppermute(last, axis, up)
        after = lax.ppermute(leading, axis, down)
        x = jnp.concatenate([before, x, after], axis=dim)
    return x


def sent_to_all(x, axis):
    peers = lax.axis_size(axis)
    return lax.all_to_all(jnp.broadcast_to(x[None], (peers, *x.shape)), axis, 0, 0, tiled=True)


def joined_along(pieces, dim):
    lengths = list(pieces.shape[1:])
    lengths[dim] *= pieces.shape[0]
    return jnp.moveaxis(pieces, 0, dim).reshape(lengths)


def gather_directly(x, axis, dim):
    pieces = sent_to_all(x, axis)
    return joined_along(pieces, dim)


def padded_to(lines, peers):
    spare = -len(lines) % peers
    return jnp.pad(lines, [(0, spare)] + [(0, 0)] * (lines.ndim - 1))


def whole_of(x, axes, dim):
    far, near = axes
    pieces = sent_to_all(sent_to_all(x, far), near)
    return joined_along(pieces.swapaxes(0, 1).reshape(-1, *x.shape), dim)


def cut_along(x, dim, peers):
    before, after = (x.shape[:dim], x.shape[dim + 1 :])
    return jnp.moveaxis(x.reshape(*before, peers, -1, *after), dim, 0)


def sent_and_summed(x, axis, dim):
    pieces = cut_along(x, dim, lax.axis_size(axis))
    arrived = lax.all_to_all(pieces, axis, split_axis=0, concat_axis=0, tiled=True)
    return arrived.sum(axis=0)


def sum_by_axis(x, axes, dim):
    far, near = axes
    own = sent_and_summed(cut_along(x, dim, lax.axis_size(far)), near, dim + 1)
    return jnp.sum(lax.all_to_all(own, far, 0, 0, tiled=True), axis=0)


def sum_by_parts(x, axes):
    padded = padded_to(x, lax.axis_size(axes[0]) * lax.axis_size(axes[1]))
    whole = whole_of(sum_by_axis(padded, axes, 0), axes, 0)
    return lax.slice_in_dim(whole, 0, len(x)).reshape(x.shape)


def together(arrays, axis):
    ends = [0]
    for a in arrays:
        ends.append(ends[-1] + a.size)
    running = sum_by_parts(jnp.concatenate([a.ravel() for a in arrays]), axis)
    return tuple((running[b:e].reshape(a.shape) for a, b, e in zip(arrays, ends, ends[1:])))


def backward_taps(weight):
    flipped = weight[::-1, ::-1, ::-1]
    return jnp.swapaxes(flipped, 3, 4)


def plane_taps(window, offset, amount, height, breadth):
    pieces = []
    for depth_tap in range(3):
        for height_tap in range(3):
            for width_tap in range(3):
                pieces.append(
                    window[
                        depth_tap,
                        offset : offset + amount,
                        height_tap : height_tap + height,
                        width_tap : width_tap + breadth,
                    ]
                )
    stacked = jnp.stack(pieces)
    return stacked.reshape(27 * amount, height * breadth)


def coarse_taps(padded, offset, amount, planes, height, breadth):
    pieces = []
    for depth_tap in range(3):
        for height_tap in range(3):
            for width_tap in range(3):
                pieces.append(
                    padded[
                        depth_tap : depth_tap + planes,
                        height_tap : height_tap + height,
                        width_tap : width_tap + breadth,
                        offset : offset + amount,
                    ]
                )
    stacked = jnp.concatenate(pieces, axis=3)
    return stacked.reshape(planes * height * breadth, 27 * amount)


def level_second(extended, weight):
    channels = weight.shape[3]
    padded = jnp.pad(extended, ((0, 0), (0, 0), (0, 0), (1, 1)))
    planes = padded.shape[0] - 2
    height = padded.shape[2] - 2
    breadth = padded.shape[3] - 2
    forward_matrix = weight.reshape(27 * channels, channels).T
    backward_matrix = backward_taps(weight).reshape(27 * channels, channels).T

    def one_plane(carried, plane_at):
        window = lax.dynamic_slice_in_dim(padded, plane_at, 3, 0)
        source = plane_taps(window, 0, channels, height, breadth)
        upstream = plane_taps(window, channels, channels, height, breadth)
        center = window[1, channels:, 1 : height + 1, 1 : breadth + 1].reshape(
            channels, height * breadth
        )
        output = jnp.dot(forward_matrix, source, preferred_element_type=jnp.float32)
        grad_in = jnp.dot(backward_matrix, upstream, preferred_element_type=jnp.float32)
        carried = carried + lax.dot_general(
            source, center, (((1,), (1,)), ((), ())), preferred_element_type=jnp.float32
        )
        output = output.astype(jnp.bfloat16).reshape(channels, height, breadth)
        grad_in = grad_in.astype(jnp.bfloat16).reshape(channels, height, breadth)
        return (carried, (output, grad_in))

    initial = jnp.zeros((27 * channels, channels), jnp.float32)
    summed, (outputs, gradients) = lax.scan(one_plane, initial, jnp.arange(planes))
    return (outputs, gradients, summed.reshape(3, 3, 3, channels, channels))


def per_device(
    middle_input, middle_cotangent, middle_weight, coarse_input, coarse_cotangent, coarse_weight
):
    middle_cells = (
        middle_input.shape[0]
        * lax.axis_size(DEPTH)
        * middle_input.shape[2]
        * lax.axis_size("height")
        * middle_input.shape[3]
    )
    coarse_cells = (
        coarse_input.shape[0]
        * lax.axis_size(DEPTH)
        * coarse_input.shape[1]
        * lax.axis_size("height")
        * coarse_input.shape[2]
    )
    middle_stack = jnp.concatenate((middle_input, middle_cotangent), axis=1)
    middle_ext = padded_2(middle_stack, ((DEPTH, 0), ("height", 2)), 1)
    middle_out, middle_dx, middle_part = level_second(middle_ext, middle_weight)
    channels = coarse_input.shape[3]
    coarse_stack = jnp.concatenate((coarse_input, coarse_cotangent), axis=3)
    coarse_ext = padded_2(coarse_stack, ((DEPTH, 0), ("height", 1)), 1)
    padded = jnp.pad(coarse_ext, ((0, 0), (0, 0), (1, 1), (0, 0)))
    planes = padded.shape[0] - 2
    height = padded.shape[1] - 2
    breadth = padded.shape[2] - 2
    turned = jnp.transpose(coarse_weight, (0, 1, 2, 4, 3))
    turned = lax.all_gather(turned, DEPTH, axis=3, tiled=True)
    full_weight = jnp.transpose(turned, (0, 1, 2, 4, 3))
    source = coarse_taps(padded, 0, channels, planes, height, breadth)
    upstream = coarse_taps(padded, channels, channels, planes, height, breadth)
    center = padded[1 : planes + 1, 1 : height + 1, 1 : breadth + 1, channels:].reshape(
        planes * height * breadth, channels
    )
    coarse_out = jnp.dot(
        source, full_weight.reshape(27 * channels, channels), preferred_element_type=jnp.float32
    )
    coarse_out = coarse_out.astype(jnp.bfloat16).reshape(planes, height, breadth, channels)
    coarse_dx = jnp.dot(
        upstream,
        backward_taps(full_weight).reshape(27 * channels, channels),
        preferred_element_type=jnp.float32,
    )
    coarse_dx = coarse_dx.astype(jnp.bfloat16).reshape(planes, height, breadth, channels)
    shard_rows = channels // lax.axis_size(DEPTH)
    partial_value = lax.dot_general(
        center, source, (((0,), (0,)), ((), ())), preferred_element_type=jnp.float32
    )
    coarse_share = lax.psum_scatter(partial_value, DEPTH, scatter_dimension=0, tiled=True)
    coarse_share = lax.psum(coarse_share, "height")
    middle_part = lax.psum(middle_part, DEPTH + ("height",))
    coarse_dw = coarse_share.T.reshape(3, 3, 3, channels, shard_rows) * (
        1.0 / math.sqrt(coarse_cells)
    )
    middle_dw = middle_part * (1.0 / math.sqrt(middle_cells))
    return (middle_out, middle_dx, middle_dw, coarse_out, coarse_dx, coarse_dw)


def solution(mesh):
    finer = Mesh(
        mesh.devices.reshape(4, 4, 2, mesh.shape["height"]),
        ("depth_0", "depth_1", "depth_2", "height"),
    )
    placed = (
        P(DEPTH, None, "height", None),
        P(DEPTH, None, "height", None),
        P(),
        P(DEPTH, "height", None, None),
        P(DEPTH, "height", None, None),
        P(None, None, None, None, DEPTH),
    )
    return jax.shard_map(
        per_device,
        mesh=finer,
        in_specs=placed,
        out_specs=(
            P(DEPTH, None, "height", None),
            P(DEPTH, None, "height", None),
            P(),
            P(DEPTH, "height", None, None),
            P(DEPTH, "height", None, None),
            P(None, None, None, None, DEPTH),
        ),
        check_vma=False,
    )
```

```python
import functools
import math

import jax
import jax.numpy as jnp
from jax import lax
from jax.experimental import pallas as pl
from jax.experimental.pallas import tpu as pltpu
from jax.sharding import PartitionSpec as P

MESH = pl.DeviceIdType.MESH
F32 = jnp.float32
BF16 = jnp.bfloat16
NT = (((1,), (1,)), ((), ()))
NN = (((1,), (0,)), ((), ()))


def dot(a, b, dims):
    return lax.dot_general(a, b, dims, preferred_element_type=F32)


def kernel(
    D,
    Z,
    middle_scale,
    coarse_scale,
    m_ref,
    wf_ref,
    wb_ref,
    xc_ref,
    gc_ref,
    gt_ref,
    ws_ref,
    mo_ref,
    mdx_ref,
    mw_ref,
    co_ref,
    cdx_ref,
    cw_ref,
    me,
    mv,
    mr,
    mrl,
    own,
    xg,
    wg,
    ggl,
    gg,
    tf,
    hr,
    gd,
    xcol,
    gcol,
    zl,
    mg,
    loc,
    ga_s,
    ga_r,
    x_s,
    x_r,
    gb_s,
    gb_r,
    w_s,
    w_r,
    ch_s,
    ch_r,
    mh_s,
    mh_r,
    mr_s,
    mr_r,
    mg_s,
    mg_r,
    ring_s,
    ring_r,
):
    d = lax.axis_index("depth")
    z = lax.axis_index("height")
    CO = 128 // D
    RB = tf.shape[1]
    n = 32 // D
    up = lax.rem(z + 1, Z)
    down = lax.rem(z + Z - 1, Z)
    after = lax.rem(d + 1, D)
    before = lax.rem(d + D - 1, D)

    barrier = pltpu.get_barrier_semaphore()

    def greet(k, carry):
        pl.semaphore_signal(
            barrier, inc=1, device_id=(lax.rem(d + k, D), z), device_id_type=MESH
        )
        return carry

    for zz in (up, down):
        for dd in (before, d, after):
            pl.semaphore_signal(barrier, inc=1, device_id=(dd, zz), device_id_type=MESH)
    lax.fori_loop(1, D, greet, 0)
    pl.semaphore_wait(barrier, D - 1 + 6)

    def remote(src, dst, s, r, to):
        return pltpu.make_async_remote_copy(
            src_ref=src, dst_ref=dst, send_sem=s, recv_sem=r, device_id=to, device_id_type=MESH
        )

    local = [
        pltpu.make_async_copy(gt_ref, ggl.at[:, 1], loc.at[0]),
        pltpu.make_async_copy(xc_ref, xg.at[d], loc.at[1]),
        pltpu.make_async_copy(ws_ref, wg.at[d], loc.at[2]),
        pltpu.make_async_copy(m_ref, me.at[1:3, 1:5], loc.at[3]),
    ]
    for c in local:
        c.start()

    ga = [
        remote(gt_ref, ggl.at[:, 0], ga_s.at[0], ga_r.at[0], (d, up)),
        remote(gt_ref, ggl.at[:, 2], ga_s.at[1], ga_r.at[1], (d, down)),
    ]
    for c in ga:
        c.start()

    mh = []
    for i, (dst, src, to) in enumerate(
        (
            (me.at[0, 1:5], m_ref.at[1], (after, z)),
            (me.at[3, 1:5], m_ref.at[0], (before, z)),
            (me.at[1:3, 0], m_ref.at[:, 3], (d, up)),
            (me.at[1:3, 5], m_ref.at[:, 0], (d, down)),
            (me.at[0, 0], m_ref.at[1, 3], (after, up)),
            (me.at[0, 5], m_ref.at[1, 0], (after, down)),
            (me.at[3, 0], m_ref.at[0, 3], (before, up)),
            (me.at[3, 5], m_ref.at[0, 0], (before, down)),
        )
    ):
        mh.append(remote(src, dst, mh_s.at[i], mh_r.at[i], to))
    for c in mh:
        c.start()

    def to_plane(src, dst, s, r):
        def one(k, carry):
            e = lax.rem(d + k, D)
            remote(src(e), dst, s, r, (e, z)).start()
            return carry

        lax.fori_loop(1, D, one, 0)

    def from_plane(whole, s, r, both=True):
        rest = whole.at[pl.ds(0, D - 1)]
        c = remote(rest, rest, s, r, (after, z))
        c.wait_recv()
        c.wait_send()

    to_plane(lambda e: xc_ref, xg.at[d], x_s, x_r)

    ch = []
    for ai, to_d in ((0, after), (1, d), (2, before)):
        for ud, to_z in ((0, up), (1, down)):
            for k, ref in ((0, xc_ref), (1, gc_ref)):
                i = (ai * 2 + ud) * 2 + k
                ch.append(
                    remote(
                        ref.at[pl.ds(64 * (1 - ud), 64)],
                        hr.at[ai, ud, k],
                        ch_s.at[i],
                        ch_r.at[i],
                        (to_d, to_z),
                    )
                )
    ch.append(remote(gc_ref, gd.at[0], ch_s.at[12], ch_r.at[12], (after, z)))
    ch.append(remote(gc_ref, gd.at[1], ch_s.at[13], ch_r.at[13], (before, z)))
    for c in ch:
        c.start()

    local[0].wait()
    for c in ga:
        c.wait()
    keep = pltpu.make_async_copy(ggl.at[d], gg.at[d], loc.at[4])
    keep.start()
    to_plane(lambda e: ggl.at[e], gg.at[d], gb_s, gb_r)
    to_plane(lambda e: ws_ref, wg.at[d], w_s, w_r)

    local[3].wait()
    for c in mh:
        c.wait()
    depth_ok = (d > 0, None, None, d < D - 1)
    height_ok = (z > 0, None, None, None, None, z < Z - 1)
    lane = lax.broadcasted_iota(jnp.int32, (64, 128), 1)
    for dd in range(4):
        for hh in range(6):
            row = me[dd, hh].astype(F32)
            for ok in (depth_ok[dd], height_ok[hh]):
                if ok is not None:
                    row = jnp.where(ok, row, 0.0)
            left = jnp.where(lane == 0, 0.0, pltpu.roll(row, 1, 1))
            right = jnp.where(lane == 127, 0.0, pltpu.roll(row, 127, 1))
            for c, v in enumerate((left, row, right)):
                v = v.astype(BF16)
                mv[dd, hh, 0, 32 * c : 32 * c + 32] = v[:32]
                mv[dd, hh, 1, 32 * c : 32 * c + 32] = v[32:]

    def columns(dd, k):
        return jnp.concatenate(
            [
                jnp.concatenate([mv[dd, h + b, k] for h in range(4)], axis=1)
                for b in range(3)
            ],
            axis=0,
        )

    seen = [
        jnp.concatenate([mv[dd + 1, h + 1, 1, 32:64] for h in range(4)], axis=1)
        for dd in range(2)
    ]
    grad = [None] * 3
    outs = [None] * 2
    for dd in range(4):
        cols = columns(dd, 0)
        part = dot(wf_ref[...], cols, NN)
        for a in range(3):
            at = dd - a
            if 0 <= at < 2:
                p = part[32 * a : 32 * a + 32]
                outs[at] = p if outs[at] is None else outs[at] + p
                g = dot(seen[at], cols, NT)
                grad[a] = g if grad[a] is None else grad[a] + g
    flat = jnp.concatenate(grad + [jnp.zeros((32, 32), F32)], axis=1)
    for ob in range(4):
        for j in range(7):
            mr[ob * 7 + j] = flat[8 * ob : 8 * ob + 8, 128 * j : 128 * j + 128]
    for t in range(28, 32):
        mr[t] = jnp.zeros((8, 128), F32)
    keep_mr = pltpu.make_async_copy(mr.at[pl.ds(d * n, n)], mrl.at[d], loc.at[5])
    keep_mr.start()
    to_plane(lambda e: mr.at[pl.ds(e * n, n)], mrl.at[d], mr_s, mr_r)
    for at in range(2):
        for h in range(4):
            mo_ref[at, h] = outs[at][:, 128 * h : 128 * h + 128].astype(BF16)
    outs = [None] * 2
    for dd in range(4):
        part = dot(wb_ref[...], columns(dd, 1), NN)
        for a in range(3):
            at = dd - a
            if 0 <= at < 2:
                p = part[32 * a : 32 * a + 32]
                outs[at] = p if outs[at] is None else outs[at] + p
    for at in range(2):
        for h in range(4):
            mdx_ref[at, h] = outs[at][:, 128 * h : 128 * h + 128].astype(BF16)

    tf[...] = jnp.zeros(tf.shape, F32)
    keep.wait()
    from_plane(gg, gb_s, gb_r)
    lanes = lax.broadcasted_iota(jnp.int32, (D, CO, 128), 2)
    first = lanes < 64
    below = jnp.where(z > 0, gg[:, 0], 0.0)
    here = gg[:, 1]
    above = jnp.where(z < Z - 1, gg[:, 2], 0.0)

    def turned(v, amount):
        return pltpu.roll(v.reshape(D * CO, 128), amount, 1).reshape(D, CO, 128)

    here_half = turned(here, 64)
    bases = (
        jnp.where(first, here_half, turned(above, 64)),
        here,
        jnp.where(first, turned(below, 64), here_half),
    )
    column = lanes % 64
    for b in range(3):
        base = bases[b]
        shifted = (
            jnp.where(column == 63, 0.0, turned(base, 127)),
            base,
            jnp.where(column == 0, 0.0, turned(base, 1)),
        )
        for c in range(3):
            at = (b * 3 + c) * CO
            tf[1 : D + 1, at : at + CO, :] = shifted[c]
    local[1].wait()
    from_plane(xg, x_s, x_r)

    def plane_pair(k, acc):
        s = 2 * k
        taps = jnp.concatenate(
            [
                tf[pl.ds(s, 3)].reshape(3 * RB, 128).astype(BF16),
                tf[pl.ds(s + 1, 3)].reshape(3 * RB, 128).astype(BF16),
            ],
            axis=1,
        )
        return acc + dot(taps, xg[pl.ds(s, 2)].reshape(256, 128), NN)

    acc = lax.fori_loop(0, D // 2, plane_pair, jnp.zeros((3 * RB, 128), F32))
    for a in range(3):
        zl[z, a * RB : (a + 1) * RB, :] = acc[(2 - a) * RB : (3 - a) * RB]
    keep_mr.wait()
    from_plane(mrl, mr_s, mr_r)
    total = mrl[0]
    for e in range(1, D):
        total = total + mrl[e]
    zl[z, 3 * RB : 3 * RB + 8 * n, :] = total.reshape(8 * n, 128)

    far = Z // 2

    def hop(way, step):
        if way == 0:
            slot = zl.at[lax.rem(z + Z - step, Z)]
            to = up
        else:
            slot = zl.at[lax.rem(z + step, Z)]
            to = down
        return remote(slot, slot, ring_s.at[way, step], ring_r.at[way, step], (d, to))

    def serve(step):
        if step > 0:
            hop(0, step - 1).wait()
            if step - 1 < far - 1:
                hop(1, step - 1).wait()
        if step < far:
            hop(0, step).start()
        if step < far - 1:
            hop(1, step).start()

    serve(0)

    for c in ch:
        c.wait()
    row_ok = (z > 0, None, z < Z - 1)
    place = lax.broadcasted_iota(jnp.int32, (256, 128), 0) % 64
    for a in range(3):
        near = jnp.clip(d + a - 1, 0, D - 1)
        for k, col in ((0, xcol), (1, gcol)):
            if k == 0:
                centre = xg[near]
            else:
                centre = gc_ref[...] if a == 1 else gd[a // 2]
            low = jnp.where(z > 0, hr[a, 0, k].astype(F32), 0.0)
            high = jnp.where(z < Z - 1, hr[a, 1, k].astype(F32), 0.0)
            rows = jnp.concatenate([low, centre.astype(F32), high], axis=0)
            if a == 0:
                rows = jnp.where(d > 0, rows, 0.0)
            if a == 2:
                rows = jnp.where(d < D - 1, rows, 0.0)
            prev = jnp.where(place == 0, 0.0, pltpu.roll(rows, 1, 0))
            nxt = jnp.where(place == 63, 0.0, pltpu.roll(rows, 255, 0))
            for c, v in enumerate((prev, rows, nxt)):
                col[a, :, 128 * c : 128 * c + 128] = v.astype(BF16)
    serve(1)
    local[2].wait()
    from_plane(wg, w_s, w_r)

    def tap(t):
        w = wg[:, t].astype(F32)
        if CO % 8:
            w = w.reshape(D // 2, 2, CO, 128)
            w = jnp.concatenate([w[:, 0], w[:, 1]], axis=1)
        return w.reshape(128, 128).astype(BF16)

    out = jnp.zeros((128, 128), F32)
    dx = jnp.zeros((128, 128), F32)
    step = 2
    for a in range(3):
        for b in range(3):
            w = [tap((a * 3 + b) * 3 + c) for c in range(3)]
            out = out + dot(xcol[a, 64 * b : 64 * b + 128, :], jnp.concatenate(w, axis=1), NT)
            dx = dx + dot(
                gcol[2 - a, 64 * (2 - b) : 64 * (2 - b) + 128, :],
                jnp.concatenate(w[::-1], axis=0),
                NN,
            )
            if step <= far:
                serve(step)
                step += 1
    co_ref[...] = out.astype(BF16)
    cdx_ref[...] = dx.astype(BF16)
    while step <= far:
        serve(step)
        step += 1

    total = zl[0]
    for s in range(1, Z):
        total = total + zl[s]
    cw_ref[...] = (total[: 3 * RB] * coarse_scale).reshape(3, RB, 128)
    own[...] = (total[3 * RB : 3 * RB + 8 * n] * middle_scale).reshape(n, 8, 128)
    keep_mg = pltpu.make_async_copy(own, mg.at[d], loc.at[6])
    keep_mg.start()
    to_plane(lambda e: own, mg.at[d], mg_s, mg_r)
    keep_mg.wait()
    from_plane(mg, mg_s, mg_r)
    mw_ref[...] = mg[...]


def per_device(D, Z, middle_input, middle_cotangent, middle_weight, coarse_input, coarse_cotangent, coarse_weight):
    CO = 128 // D
    RB = -(-9 * CO // 8) * 8
    n = 32 // D
    R = 3 * RB + 8 * n
    far = Z // 2
    middle_cells = middle_input.shape[0] * D * middle_input.shape[2] * Z * middle_input.shape[3]
    coarse_cells = coarse_input.shape[0] * D * coarse_input.shape[1] * Z * coarse_input.shape[2]
    m = jnp.concatenate(
        [jnp.swapaxes(middle_input, 1, 2), jnp.swapaxes(middle_cotangent, 1, 2)], axis=2
    )
    wf = jnp.transpose(middle_weight, (0, 4, 1, 2, 3)).reshape(96, 288)
    wb = jnp.transpose(middle_weight[::-1, ::-1, ::-1], (0, 3, 1, 2, 4)).reshape(96, 288)
    xc = coarse_input.reshape(128, 128)
    gc = coarse_cotangent.reshape(128, 128)
    gt = gc.T.astype(F32).reshape(D, CO, 128)
    ws = jnp.swapaxes(coarse_weight, 3, 4).reshape(27, CO, 128)
    dma = pltpu.SemaphoreType.DMA
    vmem = pl.BlockSpec(memory_space=pltpu.VMEM)
    mo, mdx, mw, co, cdx, cw = pl.pallas_call(
        functools.partial(
            kernel, D, Z, 1.0 / math.sqrt(middle_cells), 1.0 / math.sqrt(coarse_cells)
        ),
        out_shape=(
            jax.ShapeDtypeStruct((2, 4, 32, 128), BF16),
            jax.ShapeDtypeStruct((2, 4, 32, 128), BF16),
            jax.ShapeDtypeStruct((D, n, 8, 128), F32),
            jax.ShapeDtypeStruct((128, 128), BF16),
            jax.ShapeDtypeStruct((128, 128), BF16),
            jax.ShapeDtypeStruct((3, RB, 128), F32),
        ),
        in_specs=[vmem] * 7,
        out_specs=(vmem,) * 6,
        scratch_shapes=[
            pltpu.VMEM((4, 6, 64, 128), BF16),
            pltpu.VMEM((4, 6, 2, 96, 128), BF16),
            pltpu.VMEM((32, 8, 128), F32),
            pltpu.VMEM((D, n, 8, 128), F32),
            pltpu.VMEM((n, 8, 128), F32),
            pltpu.VMEM((D, 128, 128), BF16),
            pltpu.VMEM((D, 27, CO, 128), BF16),
            pltpu.VMEM((D, 3, CO, 128), F32),
            pltpu.VMEM((D, 3, CO, 128), F32),
            pltpu.VMEM((D + 2, RB, 128), F32),
            pltpu.VMEM((3, 2, 2, 64, 128), BF16),
            pltpu.VMEM((2, 128, 128), BF16),
            pltpu.VMEM((3, 256, 384), BF16),
            pltpu.VMEM((3, 256, 384), BF16),
            pltpu.VMEM((Z, R, 128), F32),
            pltpu.VMEM((D, n, 8, 128), F32),
            dma((7,)),
            dma((2,)),
            dma((2,)),
            dma,
            dma,
            dma,
            dma,
            dma,
            dma,
            dma((14,)),
            dma((14,)),
            dma((8,)),
            dma((8,)),
            dma,
            dma,
            dma,
            dma,
            dma((2, far)),
            dma((2, far)),
        ],
        compiler_params=pltpu.CompilerParams(collective_id=0, has_side_effects=True),
    )(m, wf, wb, xc, gc, gt, ws)
    middle_out = jnp.swapaxes(mo, 1, 2)
    middle_dx = jnp.swapaxes(mdx, 1, 2)
    tiles = mw.reshape(32, 8, 128)[:28].reshape(4, 7, 8, 128)
    flat = jnp.transpose(tiles, (0, 2, 1, 3)).reshape(32, 896)[:, :864]
    middle_dw = flat.T.reshape(3, 3, 3, 32, 32)
    coarse_dw = jnp.swapaxes(cw[:, : 9 * CO].reshape(3, 3, 3, CO, 128), 3, 4)
    return (
        middle_out,
        middle_dx,
        middle_dw,
        co.reshape(coarse_input.shape),
        cdx.reshape(coarse_input.shape),
        coarse_dw,
    )


def solution(mesh):
    placed = (
        P("depth", None, "height", None),
        P("depth", None, "height", None),
        P(),
        P("depth", "height", None, None),
        P("depth", "height", None, None),
        P(None, None, None, None, "depth"),
    )
    return jax.shard_map(
        functools.partial(per_device, mesh.shape["depth"], mesh.shape["height"]),
        mesh=mesh,
        in_specs=placed,
        out_specs=(
            placed[0],
            placed[1],
            P(),
            placed[3],
            placed[4],
            placed[5],
        ),
        check_vma=False,
    )
```

```python
import functools
import math

import jax
import jax.numpy as jnp
from jax import lax
from jax.experimental import pallas as pl
from jax.experimental.pallas import tpu as pltpu
from jax.sharding import PartitionSpec as P

MESH = pl.DeviceIdType.MESH
F32 = jnp.float32
BF16 = jnp.bfloat16
NT = (((1,), (1,)), ((), ()))
NN = (((1,), (0,)), ((), ()))


def dot(a, b, dims):
    return lax.dot_general(a, b, dims, preferred_element_type=F32)


def kernel(
    D,
    Z,
    middle_scale,
    coarse_scale,
    m_ref,
    wf_ref,
    wb_ref,
    xc_ref,
    gc_ref,
    gt_ref,
    ws_ref,
    mo_ref,
    mdx_ref,
    mw_ref,
    co_ref,
    cdx_ref,
    cw_ref,
    me,
    mv,
    mr,
    mrl,
    own,
    xg,
    wg,
    ggl,
    gg,
    tf,
    hr,
    gd,
    xcol,
    gcol,
    zl,
    mg,
    loc,
    ga_s,
    ga_r,
    x_s,
    x_r,
    xf_s,
    xf_r,
    gb_s,
    gb_r,
    w_s,
    w_r,
    wf_s,
    wf_r,
    ch_s,
    ch_r,
    mh_s,
    mh_r,
    mr_s,
    mr_r,
    mg_s,
    mg_r,
    ring_s,
    ring_r,
):
    d = lax.axis_index("depth")
    z = lax.axis_index("height")
    CO = 128 // D
    RB = tf.shape[1]
    n = 32 // D
    chip = d // 2
    core = lax.rem(d, 2)
    sibling = 2 * chip + 1 - core
    up = lax.rem(z + 1, Z)
    down = lax.rem(z + Z - 1, Z)
    after = lax.rem(d + 1, D)
    before = lax.rem(d + D - 1, D)

    barrier = pltpu.get_barrier_semaphore()

    def greet(k, carry):
        pl.semaphore_signal(
            barrier, inc=1, device_id=(lax.rem(d + k, D), z), device_id_type=MESH
        )
        return carry

    for zz in (up, down):
        for dd in (before, d, after):
            pl.semaphore_signal(barrier, inc=1, device_id=(dd, zz), device_id_type=MESH)
    lax.fori_loop(1, D, greet, 0)
    pl.semaphore_wait(barrier, D - 1 + 6)

    def remote(src, dst, s, r, to):
        return pltpu.make_async_remote_copy(
            src_ref=src, dst_ref=dst, send_sem=s, recv_sem=r, device_id=to, device_id_type=MESH
        )

    local = [
        pltpu.make_async_copy(gt_ref, ggl.at[:, 1], loc.at[0]),
        pltpu.make_async_copy(xc_ref, xg.at[chip, core], loc.at[1]),
        pltpu.make_async_copy(ws_ref, wg.at[chip, core], loc.at[2]),
        pltpu.make_async_copy(m_ref, me.at[1:3, 1:5], loc.at[3]),
    ]
    for c in local:
        c.start()

    ga = [
        remote(gt_ref, ggl.at[:, 0], ga_s.at[0], ga_r.at[0], (d, up)),
        remote(gt_ref, ggl.at[:, 2], ga_s.at[1], ga_r.at[1], (d, down)),
    ]
    for c in ga:
        c.start()

    mh = []
    for i, (dst, src, to) in enumerate(
        (
            (me.at[0, 1:5], m_ref.at[1], (after, z)),
            (me.at[3, 1:5], m_ref.at[0], (before, z)),
            (me.at[1:3, 0], m_ref.at[:, 3], (d, up)),
            (me.at[1:3, 5], m_ref.at[:, 0], (d, down)),
            (me.at[0, 0], m_ref.at[1, 3], (after, up)),
            (me.at[0, 5], m_ref.at[1, 0], (after, down)),
            (me.at[3, 0], m_ref.at[0, 3], (before, up)),
            (me.at[3, 5], m_ref.at[0, 0], (before, down)),
        )
    ):
        mh.append(remote(src, dst, mh_s.at[i], mh_r.at[i], to))
    for c in mh:
        c.start()

    def to_plane(src, dst, s, r):
        def one(k, carry):
            e = lax.rem(d + k, D)
            remote(src(e), dst, s, r, (e, z)).start()
            return carry

        lax.fori_loop(1, D, one, 0)

    def from_plane(whole, s, r, both=True):
        rest = whole.at[pl.ds(0, D - 1)]
        c = remote(rest, rest, s, r, (after, z))
        c.wait_recv()
        c.wait_send()

    def to_chips(src, dst, s, r):
        def one(k, carry):
            e = lax.rem(chip + k, D // 2)
            remote(src, dst, s, r, (2 * e + core, z)).start()
            return carry

        lax.fori_loop(1, D // 2, one, 0)

    def from_chips(whole, s, r):
        rest = whole.at[pl.ds(0, D // 2 - 1), 0]
        remote(rest, rest, s, r, (sibling, z)).wait()

    to_chips(xc_ref, xg.at[chip, core], x_s, x_r)

    ch = []
    for ai, to_d in ((0, after), (1, d), (2, before)):
        for ud, to_z in ((0, up), (1, down)):
            for k, ref in ((0, xc_ref), (1, gc_ref)):
                i = (ai * 2 + ud) * 2 + k
                ch.append(
                    remote(
                        ref.at[pl.ds(64 * (1 - ud), 64)],
                        hr.at[ai, ud, k],
                        ch_s.at[i],
                        ch_r.at[i],
                        (to_d, to_z),
                    )
                )
    ch.append(remote(gc_ref, gd.at[0], ch_s.at[12], ch_r.at[12], (after, z)))
    ch.append(remote(gc_ref, gd.at[1], ch_s.at[13], ch_r.at[13], (before, z)))
    for c in ch:
        c.start()

    local[0].wait()
    for c in ga:
        c.wait()
    keep = pltpu.make_async_copy(ggl.at[d], gg.at[d], loc.at[4])
    keep.start()
    to_plane(lambda e: ggl.at[e], gg.at[d], gb_s, gb_r)

    local[3].wait()
    for c in mh:
        c.wait()
    depth_ok = (d > 0, None, None, d < D - 1)
    height_ok = (z > 0, None, None, None, None, z < Z - 1)
    lane = lax.broadcasted_iota(jnp.int32, (64, 128), 1)
    for dd in range(4):
        for hh in range(6):
            row = me[dd, hh].astype(F32)
            for ok in (depth_ok[dd], height_ok[hh]):
                if ok is not None:
                    row = jnp.where(ok, row, 0.0)
            left = jnp.where(lane == 0, 0.0, pltpu.roll(row, 1, 1))
            right = jnp.where(lane == 127, 0.0, pltpu.roll(row, 127, 1))
            for c, v in enumerate((left, row, right)):
                v = v.astype(BF16)
                mv[dd, hh, 0, 32 * c : 32 * c + 32] = v[:32]
                mv[dd, hh, 1, 32 * c : 32 * c + 32] = v[32:]

    def columns(dd, k):
        return jnp.concatenate(
            [
                jnp.concatenate([mv[dd, h + b, k] for h in range(4)], axis=1)
                for b in range(3)
            ],
            axis=0,
        )

    seen = [
        jnp.concatenate([mv[dd + 1, h + 1, 1, 32:64] for h in range(4)], axis=1)
        for dd in range(2)
    ]
    grad = [None] * 3
    outs = [None] * 2
    for dd in range(4):
        cols = columns(dd, 0)
        part = dot(wf_ref[...], cols, NN)
        for a in range(3):
            at = dd - a
            if 0 <= at < 2:
                p = part[32 * a : 32 * a + 32]
                outs[at] = p if outs[at] is None else outs[at] + p
                g = dot(seen[at], cols, NT)
                grad[a] = g if grad[a] is None else grad[a] + g
    flat = jnp.concatenate(grad + [jnp.zeros((32, 32), F32)], axis=1)
    for ob in range(4):
        for j in range(7):
            mr[ob * 7 + j] = flat[8 * ob : 8 * ob + 8, 128 * j : 128 * j + 128]
    for t in range(28, 32):
        mr[t] = jnp.zeros((8, 128), F32)
    keep_mr = pltpu.make_async_copy(mr.at[pl.ds(d * n, n)], mrl.at[d], loc.at[5])
    keep_mr.start()
    to_plane(lambda e: mr.at[pl.ds(e * n, n)], mrl.at[d], mr_s, mr_r)
    for at in range(2):
        for h in range(4):
            mo_ref[at, h] = outs[at][:, 128 * h : 128 * h + 128].astype(BF16)
    local[1].wait()
    from_chips(xg, x_s, x_r)
    x_on = remote(xg.at[:, core], xg.at[:, core], xf_s, xf_r, (sibling, z))
    x_on.start()
    to_chips(ws_ref, wg.at[chip, core], w_s, w_r)
    outs = [None] * 2
    for dd in range(4):
        part = dot(wb_ref[...], columns(dd, 1), NN)
        for a in range(3):
            at = dd - a
            if 0 <= at < 2:
                p = part[32 * a : 32 * a + 32]
                outs[at] = p if outs[at] is None else outs[at] + p
    for at in range(2):
        for h in range(4):
            mdx_ref[at, h] = outs[at][:, 128 * h : 128 * h + 128].astype(BF16)

    tf[...] = jnp.zeros(tf.shape, F32)
    keep.wait()
    from_plane(gg, gb_s, gb_r)
    lanes = lax.broadcasted_iota(jnp.int32, (D, CO, 128), 2)
    first = lanes < 64
    below = jnp.where(z > 0, gg[:, 0].astype(F32), 0.0)
    here = gg[:, 1].astype(F32)
    above = jnp.where(z < Z - 1, gg[:, 2].astype(F32), 0.0)

    def turned(v, amount):
        return pltpu.roll(v.reshape(D * CO, 128), amount, 1).reshape(D, CO, 128)

    here_half = turned(here, 64)
    bases = (
        jnp.where(first, here_half, turned(above, 64)),
        here,
        jnp.where(first, turned(below, 64), here_half),
    )
    column = lanes % 64
    for b in range(3):
        base = bases[b]
        shifted = (
            jnp.where(column == 63, 0.0, turned(base, 127)),
            base,
            jnp.where(column == 0, 0.0, turned(base, 1)),
        )
        for c in range(3):
            at = (b * 3 + c) * CO
            tf[1 : D + 1, at : at + CO, :] = shifted[c]
    x_on.wait()

    def plane_pair(k, acc):
        s = 2 * k
        taps = jnp.concatenate(
            [
                tf[pl.ds(s, 3)].reshape(3 * RB, 128).astype(BF16),
                tf[pl.ds(s + 1, 3)].reshape(3 * RB, 128).astype(BF16),
            ],
            axis=1,
        )
        return acc + dot(taps, xg[k].reshape(256, 128), NN)

    acc = lax.fori_loop(0, D // 2, plane_pair, jnp.zeros((3 * RB, 128), F32))
    for a in range(3):
        zl[z, a * RB : (a + 1) * RB, :] = acc[(2 - a) * RB : (3 - a) * RB]
    keep_mr.wait()
    from_plane(mrl, mr_s, mr_r)
    total = mrl[0]
    for e in range(1, D):
        total = total + mrl[e]
    zl[z, 3 * RB : 3 * RB + 8 * n, :] = total.reshape(8 * n, 128)

    far = Z // 2

    part = zl.shape[1] // 4

    def hop(way, step, q):
        if way == 0:
            slot = lax.rem(z + Z - step, Z)
            to = up
        else:
            slot = lax.rem(z + step, Z)
            to = down
        rows = zl.at[slot, pl.ds(part * q, part)]
        return remote(
            rows, rows, ring_s.at[way, q, step], ring_r.at[way, q, step], (d, to)
        )

    last = (far, far - 1)

    def serve(step):
        for q in range(4):
            for way in range(2):
                if 0 < step <= last[way]:
                    hop(way, step - 1, q).wait_recv()
                if step < last[way]:
                    hop(way, step, q).start()

    serve(0)

    for c in ch:
        c.wait()
    row_ok = (z > 0, None, z < Z - 1)
    place = lax.broadcasted_iota(jnp.int32, (256, 128), 0) % 64
    for a in range(3):
        near = jnp.clip(d + a - 1, 0, D - 1)
        for k, col in ((0, xcol), (1, gcol)):
            if k == 0:
                centre = xg[near // 2, lax.rem(near, 2)]
            else:
                centre = gc_ref[...] if a == 1 else gd[a // 2]
            low = jnp.where(z > 0, hr[a, 0, k].astype(F32), 0.0)
            high = jnp.where(z < Z - 1, hr[a, 1, k].astype(F32), 0.0)
            rows = jnp.concatenate([low, centre.astype(F32), high], axis=0)
            if a == 0:
                rows = jnp.where(d > 0, rows, 0.0)
            if a == 2:
                rows = jnp.where(d < D - 1, rows, 0.0)
            prev = jnp.where(place == 0, 0.0, pltpu.roll(rows, 1, 0))
            nxt = jnp.where(place == 63, 0.0, pltpu.roll(rows, 255, 0))
            for c, v in enumerate((prev, rows, nxt)):
                col[a, :, 128 * c : 128 * c + 128] = v.astype(BF16)
    serve(1)
    local[2].wait()
    from_chips(wg, w_s, w_r)
    w_on = remote(wg.at[:, core], wg.at[:, core], wf_s, wf_r, (sibling, z))
    w_on.start()
    for step in range(2, far + 1):
        serve(step)

    total = zl[0]
    for s in range(1, Z):
        total = total + zl[s]
    cw_ref[...] = (total[: 3 * RB] * coarse_scale).reshape(3, RB, 128)
    own[...] = (total[3 * RB : 3 * RB + 8 * n] * middle_scale).reshape(n, 8, 128)
    keep_mg = pltpu.make_async_copy(own, mg.at[d], loc.at[6])
    keep_mg.start()
    to_plane(lambda e: own, mg.at[d], mg_s, mg_r)
    w_on.wait()

    def tap(t):
        w = wg[:, :, t].astype(F32)
        if CO % 8:
            w = jnp.concatenate([w[:, 0], w[:, 1]], axis=1)
        return w.reshape(128, 128).astype(BF16)

    out = jnp.zeros((128, 128), F32)
    dx = jnp.zeros((128, 128), F32)
    for a in range(3):
        for b in range(3):
            w = [tap((a * 3 + b) * 3 + c) for c in range(3)]
            out = out + dot(xcol[a, 64 * b : 64 * b + 128, :], jnp.concatenate(w, axis=1), NT)
            dx = dx + dot(
                gcol[2 - a, 64 * (2 - b) : 64 * (2 - b) + 128, :],
                jnp.concatenate(w[::-1], axis=0),
                NN,
            )
    co_ref[...] = out.astype(BF16)
    cdx_ref[...] = dx.astype(BF16)
    for step in range(far):
        for q in range(4):
            for way in range(2):
                if step < last[way]:
                    hop(way, step, q).wait_send()
    keep_mg.wait()
    from_plane(mg, mg_s, mg_r)
    mw_ref[...] = mg[...]


def per_device(D, Z, middle_input, middle_cotangent, middle_weight, coarse_input, coarse_cotangent, coarse_weight):
    CO = 128 // D
    RB = -(-9 * CO // 8) * 8
    n = 32 // D
    R = 3 * RB + 8 * n
    far = Z // 2
    middle_cells = middle_input.shape[0] * D * middle_input.shape[2] * Z * middle_input.shape[3]
    coarse_cells = coarse_input.shape[0] * D * coarse_input.shape[1] * Z * coarse_input.shape[2]
    m = jnp.concatenate(
        [jnp.swapaxes(middle_input, 1, 2), jnp.swapaxes(middle_cotangent, 1, 2)], axis=2
    )
    wf = jnp.transpose(middle_weight, (0, 4, 1, 2, 3)).reshape(96, 288)
    wb = jnp.transpose(middle_weight[::-1, ::-1, ::-1], (0, 3, 1, 2, 4)).reshape(96, 288)
    xc = coarse_input.reshape(128, 128)
    gc = coarse_cotangent.reshape(128, 128)
    gt = gc.T.reshape(D, CO, 128)
    ws = jnp.swapaxes(coarse_weight, 3, 4).reshape(27, CO, 128)
    dma = pltpu.SemaphoreType.DMA
    vmem = pl.BlockSpec(memory_space=pltpu.VMEM)
    mo, mdx, mw, co, cdx, cw = pl.pallas_call(
        functools.partial(
            kernel, D, Z, 1.0 / math.sqrt(middle_cells), 1.0 / math.sqrt(coarse_cells)
        ),
        out_shape=(
            jax.ShapeDtypeStruct((2, 4, 32, 128), BF16),
            jax.ShapeDtypeStruct((2, 4, 32, 128), BF16),
            jax.ShapeDtypeStruct((D, n, 8, 128), F32),
            jax.ShapeDtypeStruct((128, 128), BF16),
            jax.ShapeDtypeStruct((128, 128), BF16),
            jax.ShapeDtypeStruct((3, RB, 128), F32),
        ),
        in_specs=[vmem] * 7,
        out_specs=(vmem,) * 6,
        scratch_shapes=[
            pltpu.VMEM((4, 6, 64, 128), BF16),
            pltpu.VMEM((4, 6, 2, 96, 128), BF16),
            pltpu.VMEM((32, 8, 128), F32),
            pltpu.VMEM((D, n, 8, 128), F32),
            pltpu.VMEM((n, 8, 128), F32),
            pltpu.VMEM((D // 2, 2, 128, 128), BF16),
            pltpu.VMEM((D // 2, 2, 27, CO, 128), BF16),
            pltpu.VMEM((D, 3, CO, 128), BF16),
            pltpu.VMEM((D, 3, CO, 128), BF16),
            pltpu.VMEM((D + 2, RB, 128), F32),
            pltpu.VMEM((3, 2, 2, 64, 128), BF16),
            pltpu.VMEM((2, 128, 128), BF16),
            pltpu.VMEM((3, 256, 384), BF16),
            pltpu.VMEM((3, 256, 384), BF16),
            pltpu.VMEM((Z, R, 128), F32),
            pltpu.VMEM((D, n, 8, 128), F32),
            dma((7,)),
            dma((2,)),
            dma((2,)),
            dma,
            dma,
            dma,
            dma,
            dma,
            dma,
            dma,
            dma,
            dma,
            dma,
            dma((14,)),
            dma((14,)),
            dma((8,)),
            dma((8,)),
            dma,
            dma,
            dma,
            dma,
            dma((2, 4, far)),
            dma((2, 4, far)),
        ],
        compiler_params=pltpu.CompilerParams(collective_id=0, has_side_effects=True),
    )(m, wf, wb, xc, gc, gt, ws)
    middle_out = jnp.swapaxes(mo, 1, 2)
    middle_dx = jnp.swapaxes(mdx, 1, 2)
    tiles = mw.reshape(32, 8, 128)[:28].reshape(4, 7, 8, 128)
    flat = jnp.transpose(tiles, (0, 2, 1, 3)).reshape(32, 896)[:, :864]
    middle_dw = flat.T.reshape(3, 3, 3, 32, 32)
    coarse_dw = jnp.swapaxes(cw[:, : 9 * CO].reshape(3, 3, 3, CO, 128), 3, 4)
    return (
        middle_out,
        middle_dx,
        middle_dw,
        co.reshape(coarse_input.shape),
        cdx.reshape(coarse_input.shape),
        coarse_dw,
    )


def solution(mesh):
    placed = (
        P("depth", None, "height", None),
        P("depth", None, "height", None),
        P(),
        P("depth", "height", None, None),
        P("depth", "height", None, None),
        P(None, None, None, None, "depth"),
    )
    return jax.shard_map(
        functools.partial(per_device, mesh.shape["depth"], mesh.shape["height"]),
        mesh=mesh,
        in_specs=placed,
        out_specs=(
            placed[0],
            placed[1],
            P(),
            placed[3],
            placed[4],
            placed[5],
        ),
        check_vma=False,
    )
```

```python
import functools
import math

import jax
import jax.numpy as jnp
from jax import lax
from jax.experimental import pallas as pl
from jax.experimental.pallas import tpu as pltpu
from jax.sharding import PartitionSpec as P

MESH = pl.DeviceIdType.MESH
F32 = jnp.float32
BF16 = jnp.bfloat16
NT = (((1,), (1,)), ((), ()))
NN = (((1,), (0,)), ((), ()))


def dot(a, b, dims):
    return lax.dot_general(a, b, dims, preferred_element_type=F32)


def kernel(
    D,
    Z,
    middle_scale,
    coarse_scale,
    mi_ref,
    mc_ref,
    mk_ref,
    xc_ref,
    gc_ref,
    gt_ref,
    ws_ref,
    mo_ref,
    mdx_ref,
    mw_ref,
    co_ref,
    cdx_ref,
    cw_ref,
    me,
    mv,
    mr,
    mrl,
    own,
    xg,
    wg,
    ggl,
    gg,
    tf,
    hr,
    gd,
    xcol,
    gcol,
    zl,
    zm,
    mg,
    loc,
    ga_s,
    ga_r,
    x_s,
    x_r,
    xf_s,
    xf_r,
    gb_s,
    gb_r,
    w_s,
    w_r,
    wf_s,
    wf_r,
    ch_s,
    ch_r,
    mh_s,
    mh_r,
    mr_s,
    mr_r,
    mg_s,
    mg_r,
    ring_s,
    ring_r,
    turn_s,
    turn_r,
):
    d = lax.axis_index("depth")
    z = lax.axis_index("height")
    CO = 128 // D
    RB = tf.shape[1]
    n = 32 // D
    chip = d // 2
    core = lax.rem(d, 2)
    sibling = 2 * chip + 1 - core
    up = lax.rem(z + 1, Z)
    down = lax.rem(z + Z - 1, Z)
    after = lax.rem(d + 1, D)
    before = lax.rem(d + D - 1, D)

    barrier = pltpu.get_barrier_semaphore()

    def greet(k, carry):
        pl.semaphore_signal(
            barrier, inc=1, device_id=(lax.rem(d + k, D), z), device_id_type=MESH
        )
        return carry

    for zz in (up, down):
        for dd in (before, d, after):
            pl.semaphore_signal(barrier, inc=1, device_id=(dd, zz), device_id_type=MESH)
    lax.fori_loop(1, D, greet, 0)

    taps = [mk_ref[t].astype(F32) for t in range(27)]
    forward = jnp.concatenate(
        [
            jnp.concatenate([taps[9 * a + t].T for t in range(9)], axis=1)
            for a in range(3)
        ],
        axis=0,
    ).astype(BF16)
    backward = jnp.concatenate(
        [
            jnp.concatenate([taps[26 - 9 * a - t] for t in range(9)], axis=1)
            for a in range(3)
        ],
        axis=0,
    ).astype(BF16)
    pl.semaphore_wait(barrier, D - 1 + 6)

    def remote(src, dst, s, r, to):
        return pltpu.make_async_remote_copy(
            src_ref=src, dst_ref=dst, send_sem=s, recv_sem=r, device_id=to, device_id_type=MESH
        )

    local = [
        pltpu.make_async_copy(gt_ref, ggl.at[:, 1], loc.at[0]),
        pltpu.make_async_copy(xc_ref, xg.at[chip, core], loc.at[1]),
        pltpu.make_async_copy(ws_ref, wg.at[chip, core], loc.at[2]),
        pltpu.make_async_copy(mi_ref, me.at[1:3, 1:5, 0:32], loc.at[3]),
        pltpu.make_async_copy(mc_ref, me.at[1:3, 1:5, 32:64], loc.at[7]),
    ]
    for c in local:
        c.start()

    ga = [
        remote(gt_ref, ggl.at[:, 0], ga_s.at[0], ga_r.at[0], (d, up)),
        remote(gt_ref, ggl.at[:, 2], ga_s.at[1], ga_r.at[1], (d, down)),
    ]
    for c in ga:
        c.start()

    mh = []
    for k, ref in ((0, mi_ref), (1, mc_ref)):
        part = slice(32 * k, 32 * k + 32)
        for i, (dst, src, to) in enumerate(
            (
                (me.at[0, 1:5, part], ref.at[1], (after, z)),
                (me.at[3, 1:5, part], ref.at[0], (before, z)),
                (me.at[1:3, 0, part], ref.at[:, 3], (d, up)),
                (me.at[1:3, 5, part], ref.at[:, 0], (d, down)),
                (me.at[0, 0, part], ref.at[1, 3], (after, up)),
                (me.at[0, 5, part], ref.at[1, 0], (after, down)),
                (me.at[3, 0, part], ref.at[0, 3], (before, up)),
                (me.at[3, 5, part], ref.at[0, 0], (before, down)),
            )
        ):
            mh.append(remote(src, dst, mh_s.at[k, i], mh_r.at[k, i], to))
    for c in mh:
        c.start()

    def to_plane(src, dst, s, r):
        def one(k, carry):
            e = lax.rem(d + k, D)
            remote(src(e), dst, s, r, (e, z)).start()
            return carry

        lax.fori_loop(1, D, one, 0)

    def from_plane(whole, s, r, both=True):
        rest = whole.at[pl.ds(0, D - 1)]
        c = remote(rest, rest, s, r, (after, z))
        c.wait_recv()
        c.wait_send()

    def to_chips(src, dst, s, r):
        def one(k, carry):
            e = lax.rem(chip + k, D // 2)
            remote(src, dst, s, r, (2 * e + core, z)).start()
            return carry

        lax.fori_loop(1, D // 2, one, 0)

    def from_chips(whole, s, r):
        rest = whole.at[pl.ds(0, D // 2 - 1), 0]
        remote(rest, rest, s, r, (sibling, z)).wait()

    to_chips(xc_ref, xg.at[chip, core], x_s, x_r)

    ch = []
    for ai, to_d in ((0, after), (1, d), (2, before)):
        for ud, to_z in ((0, up), (1, down)):
            for k, ref in ((0, xc_ref), (1, gc_ref)):
                i = (ai * 2 + ud) * 2 + k
                ch.append(
                    remote(
                        ref.at[pl.ds(64 * (1 - ud), 64)],
                        hr.at[ai, ud, k],
                        ch_s.at[i],
                        ch_r.at[i],
                        (to_d, to_z),
                    )
                )
    ch.append(remote(gc_ref, gd.at[0], ch_s.at[12], ch_r.at[12], (after, z)))
    ch.append(remote(gc_ref, gd.at[1], ch_s.at[13], ch_r.at[13], (before, z)))
    for c in ch:
        c.start()

    local[0].wait()
    for c in ga:
        c.wait()
    keep = pltpu.make_async_copy(ggl.at[d], gg.at[d], loc.at[4])
    keep.start()
    to_plane(lambda e: ggl.at[e], gg.at[d], gb_s, gb_r)

    local[3].wait()
    local[4].wait()
    for c in mh:
        c.wait()
    depth_ok = (d > 0, None, None, d < D - 1)
    height_ok = (z > 0, None, None, None, None, z < Z - 1)
    lane = lax.broadcasted_iota(jnp.int32, (64, 128), 1)
    for dd in range(4):
        for hh in range(6):
            row = me[dd, hh].astype(F32)
            for ok in (depth_ok[dd], height_ok[hh]):
                if ok is not None:
                    row = jnp.where(ok, row, 0.0)
            left = jnp.where(lane == 0, 0.0, pltpu.roll(row, 1, 1))
            right = jnp.where(lane == 127, 0.0, pltpu.roll(row, 127, 1))
            for c, v in enumerate((left, row, right)):
                v = v.astype(BF16)
                mv[dd, hh, 0, 32 * c : 32 * c + 32] = v[:32]
                mv[dd, hh, 1, 32 * c : 32 * c + 32] = v[32:]

    def columns(dd, k):
        return jnp.concatenate(
            [
                jnp.concatenate([mv[dd, h + b, k] for h in range(4)], axis=1)
                for b in range(3)
            ],
            axis=0,
        )

    seen = [
        jnp.concatenate([mv[dd + 1, h + 1, 1, 32:64] for h in range(4)], axis=1)
        for dd in range(2)
    ]
    grad = [None] * 3
    outs = [None] * 2
    for dd in range(4):
        cols = columns(dd, 0)
        part = dot(forward, cols, NN)
        for a in range(3):
            at = dd - a
            if 0 <= at < 2:
                p = part[32 * a : 32 * a + 32]
                outs[at] = p if outs[at] is None else outs[at] + p
                g = dot(seen[at], cols, NT)
                grad[a] = g if grad[a] is None else grad[a] + g
    flat = jnp.concatenate(grad + [jnp.zeros((32, 32), F32)], axis=1)
    for ob in range(4):
        for j in range(7):
            mr[ob * 7 + j] = flat[8 * ob : 8 * ob + 8, 128 * j : 128 * j + 128]
    for t in range(28, 32):
        mr[t] = jnp.zeros((8, 128), F32)
    keep_mr = pltpu.make_async_copy(mr.at[pl.ds(d * n, n)], mrl.at[d], loc.at[5])
    keep_mr.start()
    to_plane(lambda e: mr.at[pl.ds(e * n, n)], mrl.at[d], mr_s, mr_r)
    for at in range(2):
        for h in range(4):
            mo_ref[at, h] = outs[at][:, 128 * h : 128 * h + 128].astype(BF16)
    local[1].wait()
    from_chips(xg, x_s, x_r)
    x_on = remote(xg.at[:, core], xg.at[:, core], xf_s, xf_r, (sibling, z))
    x_on.start()
    to_chips(ws_ref, wg.at[chip, core], w_s, w_r)
    far = Z // 2

    third = zl.shape[1] // 3

    def hop(way, step, q):
        if way == 0:
            slot = lax.rem(z + Z - step, Z)
            to = up
        else:
            slot = lax.rem(z + step, Z)
            to = down
        rows = zl.at[slot, pl.ds(third * q, third)]
        return remote(
            rows, rows, ring_s.at[way, q, step], ring_r.at[way, q, step], (d, to)
        )

    last = (far, far - 1)

    def serve(step):
        for q in range(3):
            for way in range(2):
                if 0 < step <= last[way]:
                    hop(way, step - 1, q).wait_recv()
                if step < last[way]:
                    hop(way, step, q).start()

    def turn(way, step):
        slot = lax.rem(z + Z - step, Z) if way == 0 else lax.rem(z + step, Z)
        rows = zm.at[slot]
        to = down if way else up
        return remote(rows, rows, turn_s.at[way, step], turn_r.at[way, step], (d, to))

    def serve_middle(step):
        for way in range(2):
            if 0 < step <= last[way]:
                turn(way, step - 1).wait_recv()
            if step < last[way]:
                turn(way, step).start()

    keep_mr.wait()
    from_plane(mrl, mr_s, mr_r)
    total = mrl[0]
    for e in range(1, D):
        total = total + mrl[e]
    zm[z] = total.reshape(8 * n, 128)
    served = []
    last_gather = pltpu.make_async_copy(own, mg.at[d], loc.at[6])

    def advance():
        step = len(served)
        if step > far:
            return
        served.append(step)
        serve_middle(step)
        if step == far:
            whole = zm[0]
            for s in range(1, Z):
                whole = whole + zm[s]
            own[...] = (whole * middle_scale).reshape(n, 8, 128)
            last_gather.start()
            to_plane(lambda e: own, mg.at[d], mg_s, mg_r)

    advance()
    outs = [None] * 2
    for dd in range(4):
        part = dot(backward, columns(dd, 1), NN)
        for a in range(3):
            at = dd - a
            if 0 <= at < 2:
                p = part[32 * a : 32 * a + 32]
                outs[at] = p if outs[at] is None else outs[at] + p
    for at in range(2):
        for h in range(4):
            mdx_ref[at, h] = outs[at][:, 128 * h : 128 * h + 128].astype(BF16)

    advance()

    tf[...] = jnp.zeros(tf.shape, F32)
    keep.wait()
    from_plane(gg, gb_s, gb_r)
    lanes = lax.broadcasted_iota(jnp.int32, (D, CO, 128), 2)
    first = lanes < 64
    below = jnp.where(z > 0, gg[:, 0].astype(F32), 0.0)
    here = gg[:, 1].astype(F32)
    above = jnp.where(z < Z - 1, gg[:, 2].astype(F32), 0.0)

    def turned(v, amount):
        return pltpu.roll(v.reshape(D * CO, 128), amount, 1).reshape(D, CO, 128)

    here_half = turned(here, 64)
    bases = (
        jnp.where(first, here_half, turned(above, 64)),
        here,
        jnp.where(first, turned(below, 64), here_half),
    )
    column = lanes % 64
    for b in range(3):
        base = bases[b]
        shifted = (
            jnp.where(column == 63, 0.0, turned(base, 127)),
            base,
            jnp.where(column == 0, 0.0, turned(base, 1)),
        )
        for c in range(3):
            at = (b * 3 + c) * CO
            tf[1 : D + 1, at : at + CO, :] = shifted[c]
    advance()
    x_on.wait()

    def plane_pair(k, acc):
        s = 2 * k
        taps = jnp.concatenate(
            [
                tf[pl.ds(s, 3)].reshape(3 * RB, 128).astype(BF16),
                tf[pl.ds(s + 1, 3)].reshape(3 * RB, 128).astype(BF16),
            ],
            axis=1,
        )
        return acc + dot(taps, xg[k].reshape(256, 128), NN)

    acc = lax.fori_loop(0, D // 2, plane_pair, jnp.zeros((3 * RB, 128), F32))
    for a in range(3):
        zl[z, a * RB : (a + 1) * RB, :] = acc[(2 - a) * RB : (3 - a) * RB]

    serve(0)
    advance()

    for c in ch:
        c.wait()
    row_ok = (z > 0, None, z < Z - 1)
    place = lax.broadcasted_iota(jnp.int32, (256, 128), 0) % 64
    for a in range(3):
        near = jnp.clip(d + a - 1, 0, D - 1)
        for k, col in ((0, xcol), (1, gcol)):
            if k == 0:
                centre = xg[near // 2, lax.rem(near, 2)]
            else:
                centre = gc_ref[...] if a == 1 else gd[a // 2]
            low = jnp.where(z > 0, hr[a, 0, k].astype(F32), 0.0)
            high = jnp.where(z < Z - 1, hr[a, 1, k].astype(F32), 0.0)
            rows = jnp.concatenate([low, centre.astype(F32), high], axis=0)
            if a == 0:
                rows = jnp.where(d > 0, rows, 0.0)
            if a == 2:
                rows = jnp.where(d < D - 1, rows, 0.0)
            prev = jnp.where(place == 0, 0.0, pltpu.roll(rows, 1, 0))
            nxt = jnp.where(place == 63, 0.0, pltpu.roll(rows, 255, 0))
            for c, v in enumerate((prev, rows, nxt)):
                col[a, :, 128 * c : 128 * c + 128] = v.astype(BF16)
    serve(1)
    advance()
    local[2].wait()
    from_chips(wg, w_s, w_r)
    w_on = remote(wg.at[:, core], wg.at[:, core], wf_s, wf_r, (sibling, z))
    w_on.start()
    for step in range(2, far + 1):
        serve(step)
        advance()

    total = zl[0]
    for s in range(1, Z):
        total = total + zl[s]
    cw_ref[...] = (total * coarse_scale).reshape(3, RB, 128)
    w_on.wait()

    def tap(t):
        w = wg[:, :, t].astype(F32)
        if CO % 8:
            w = jnp.concatenate([w[:, 0], w[:, 1]], axis=1)
        return w.reshape(128, 128).astype(BF16)

    out = jnp.zeros((128, 128), F32)
    dx = jnp.zeros((128, 128), F32)
    for a in range(3):
        for b in range(3):
            w = [tap((a * 3 + b) * 3 + c) for c in range(3)]
            out = out + dot(xcol[a, 64 * b : 64 * b + 128, :], jnp.concatenate(w, axis=1), NT)
            dx = dx + dot(
                gcol[2 - a, 64 * (2 - b) : 64 * (2 - b) + 128, :],
                jnp.concatenate(w[::-1], axis=0),
                NN,
            )
    co_ref[...] = out.astype(BF16)
    cdx_ref[...] = dx.astype(BF16)
    for step in range(far):
        for q in range(3):
            for way in range(2):
                if step < last[way]:
                    hop(way, step, q).wait_send()
    for step in range(far):
        for way in range(2):
            if step < last[way]:
                turn(way, step).wait_send()
    last_gather.wait()
    from_plane(mg, mg_s, mg_r)
    mw_ref[...] = mg[...]


def per_device(D, Z, middle_input, middle_cotangent, middle_weight, coarse_input, coarse_cotangent, coarse_weight):
    CO = 128 // D
    RB = -(-9 * CO // 8) * 8
    n = 32 // D
    R = 3 * RB
    far = Z // 2
    middle_cells = middle_input.shape[0] * D * middle_input.shape[2] * Z * middle_input.shape[3]
    coarse_cells = coarse_input.shape[0] * D * coarse_input.shape[1] * Z * coarse_input.shape[2]
    mi = jnp.swapaxes(middle_input, 1, 2)
    mc = jnp.swapaxes(middle_cotangent, 1, 2)
    mk = middle_weight.reshape(27, 32, 32)
    xc = coarse_input.reshape(128, 128)
    gc = coarse_cotangent.reshape(128, 128)
    gt = gc.T.reshape(D, CO, 128)
    ws = jnp.swapaxes(coarse_weight, 3, 4).reshape(27, CO, 128)
    dma = pltpu.SemaphoreType.DMA
    vmem = pl.BlockSpec(memory_space=pltpu.VMEM)
    mo, mdx, mw, co, cdx, cw = pl.pallas_call(
        functools.partial(
            kernel, D, Z, 1.0 / math.sqrt(middle_cells), 1.0 / math.sqrt(coarse_cells)
        ),
        out_shape=(
            jax.ShapeDtypeStruct((2, 4, 32, 128), BF16),
            jax.ShapeDtypeStruct((2, 4, 32, 128), BF16),
            jax.ShapeDtypeStruct((D, n, 8, 128), F32),
            jax.ShapeDtypeStruct((128, 128), BF16),
            jax.ShapeDtypeStruct((128, 128), BF16),
            jax.ShapeDtypeStruct((3, RB, 128), F32),
        ),
        in_specs=[vmem] * 7,
        out_specs=(vmem,) * 6,
        scratch_shapes=[
            pltpu.VMEM((4, 6, 64, 128), BF16),
            pltpu.VMEM((4, 6, 2, 96, 128), BF16),
            pltpu.VMEM((32, 8, 128), F32),
            pltpu.VMEM((D, n, 8, 128), F32),
            pltpu.VMEM((n, 8, 128), F32),
            pltpu.VMEM((D // 2, 2, 128, 128), BF16),
            pltpu.VMEM((D // 2, 2, 27, CO, 128), BF16),
            pltpu.VMEM((D, 3, CO, 128), BF16),
            pltpu.VMEM((D, 3, CO, 128), BF16),
            pltpu.VMEM((D + 2, RB, 128), F32),
            pltpu.VMEM((3, 2, 2, 64, 128), BF16),
            pltpu.VMEM((2, 128, 128), BF16),
            pltpu.VMEM((3, 256, 384), BF16),
            pltpu.VMEM((3, 256, 384), BF16),
            pltpu.VMEM((Z, R, 128), F32),
            pltpu.VMEM((Z, 8 * n, 128), F32),
            pltpu.VMEM((D, n, 8, 128), F32),
            dma((8,)),
            dma((2,)),
            dma((2,)),
            dma,
            dma,
            dma,
            dma,
            dma,
            dma,
            dma,
            dma,
            dma,
            dma,
            dma((14,)),
            dma((14,)),
            dma((2, 8)),
            dma((2, 8)),
            dma,
            dma,
            dma,
            dma,
            dma((2, 3, far)),
            dma((2, 3, far)),
            dma((2, far)),
            dma((2, far)),
        ],
        compiler_params=pltpu.CompilerParams(collective_id=0, has_side_effects=True),
    )(mi, mc, mk, xc, gc, gt, ws)
    middle_out = jnp.swapaxes(mo, 1, 2)
    middle_dx = jnp.swapaxes(mdx, 1, 2)
    tiles = mw.reshape(32, 8, 128)[:28].reshape(4, 7, 8, 128)
    flat = jnp.transpose(tiles, (0, 2, 1, 3)).reshape(32, 896)[:, :864]
    middle_dw = flat.T.reshape(3, 3, 3, 32, 32)
    coarse_dw = jnp.swapaxes(cw[:, : 9 * CO].reshape(3, 3, 3, CO, 128), 3, 4)
    return (
        middle_out,
        middle_dx,
        middle_dw,
        co.reshape(coarse_input.shape),
        cdx.reshape(coarse_input.shape),
        coarse_dw,
    )


def solution(mesh):
    placed = (
        P("depth", None, "height", None),
        P("depth", None, "height", None),
        P(),
        P("depth", "height", None, None),
        P("depth", "height", None, None),
        P(None, None, None, None, "depth"),
    )
    return jax.shard_map(
        functools.partial(per_device, mesh.shape["depth"], mesh.shape["height"]),
        mesh=mesh,
        in_specs=placed,
        out_specs=(
            placed[0],
            placed[1],
            P(),
            placed[3],
            placed[4],
            placed[5],
        ),
        check_vma=False,
    )
```

```python
import functools
import math

import jax
import jax.numpy as jnp
from jax import lax
from jax.experimental import pallas as pl
from jax.experimental.pallas import tpu as pltpu
from jax.sharding import PartitionSpec as P

MESH = pl.DeviceIdType.MESH
F32 = jnp.float32
BF16 = jnp.bfloat16
NT = (((1,), (1,)), ((), ()))
NN = (((1,), (0,)), ((), ()))


def dot(a, b, dims):
    return lax.dot_general(a, b, dims, preferred_element_type=F32)


def kernel(
    D,
    Z,
    middle_scale,
    coarse_scale,
    mi_ref,
    mc_ref,
    mk_ref,
    xc_ref,
    gc_ref,
    gt_ref,
    ws_ref,
    mo_ref,
    mdx_ref,
    mw_ref,
    co_ref,
    cdx_ref,
    cw_ref,
    me,
    mv,
    mr,
    mrl,
    own,
    xg,
    wg,
    ggl,
    gg,
    tf,
    hr,
    gd,
    xcol,
    gcol,
    za,
    zp,
    zl,
    fin,
    zm,
    mg,
    loc,
    ga_s,
    ga_r,
    x_s,
    x_r,
    xf_s,
    xf_r,
    gb_s,
    gb_r,
    w_s,
    w_r,
    wf_s,
    wf_r,
    ch_s,
    ch_r,
    mh_s,
    mh_r,
    mr_s,
    mr_r,
    mg_s,
    mg_r,
    ring_s,
    ring_r,
    turn_s,
    turn_r,
    pair_s,
    pair_r,
):
    d = lax.axis_index("depth")
    z = lax.axis_index("height")
    CO = 128 // D
    RB = tf.shape[1]
    n = 32 // D
    chip = d // 2
    core = lax.rem(d, 2)
    sibling = 2 * chip + 1 - core
    up = lax.rem(z + 1, Z)
    down = lax.rem(z + Z - 1, Z)
    after = lax.rem(d + 1, D)
    before = lax.rem(d + D - 1, D)
    up_two = lax.rem(z + 2, Z)
    down_two = lax.rem(z + Z - 2, Z)
    pair = z // 2
    side = lax.rem(z, 2)
    other = z + 1 - 2 * side

    barrier = pltpu.get_barrier_semaphore()

    def greet(k, carry):
        pl.semaphore_signal(
            barrier, inc=1, device_id=(lax.rem(d + k, D), z), device_id_type=MESH
        )
        return carry

    for zz in (up, down):
        for dd in (before, d, after):
            pl.semaphore_signal(barrier, inc=1, device_id=(dd, zz), device_id_type=MESH)
    for zz in (up_two, down_two):
        pl.semaphore_signal(barrier, inc=1, device_id=(d, zz), device_id_type=MESH)
    lax.fori_loop(1, D, greet, 0)

    taps = [mk_ref[t].astype(F32) for t in range(27)]
    forward = jnp.concatenate(
        [
            jnp.concatenate([taps[9 * a + t].T for t in range(9)], axis=1)
            for a in range(3)
        ],
        axis=0,
    ).astype(BF16)
    backward = jnp.concatenate(
        [
            jnp.concatenate([taps[26 - 9 * a - t] for t in range(9)], axis=1)
            for a in range(3)
        ],
        axis=0,
    ).astype(BF16)
    pl.semaphore_wait(barrier, D - 1 + 8)

    def remote(src, dst, s, r, to):
        return pltpu.make_async_remote_copy(
            src_ref=src, dst_ref=dst, send_sem=s, recv_sem=r, device_id=to, device_id_type=MESH
        )

    local = [
        pltpu.make_async_copy(gt_ref, ggl.at[:, 1], loc.at[0]),
        pltpu.make_async_copy(xc_ref, xg.at[chip, core], loc.at[1]),
        pltpu.make_async_copy(ws_ref, wg.at[chip, core], loc.at[2]),
        pltpu.make_async_copy(mi_ref, me.at[1:3, 1:5, 0:32], loc.at[3]),
        pltpu.make_async_copy(mc_ref, me.at[1:3, 1:5, 32:64], loc.at[7]),
    ]
    for c in local:
        c.start()

    ga = [
        remote(gt_ref, ggl.at[:, 0], ga_s.at[0], ga_r.at[0], (d, up)),
        remote(gt_ref, ggl.at[:, 2], ga_s.at[1], ga_r.at[1], (d, down)),
    ]
    for c in ga:
        c.start()

    mh = []
    for k, ref in ((0, mi_ref), (1, mc_ref)):
        part = slice(32 * k, 32 * k + 32)
        for i, (dst, src, to) in enumerate(
            (
                (me.at[0, 1:5, part], ref.at[1], (after, z)),
                (me.at[3, 1:5, part], ref.at[0], (before, z)),
                (me.at[1:3, 0, part], ref.at[:, 3], (d, up)),
                (me.at[1:3, 5, part], ref.at[:, 0], (d, down)),
                (me.at[0, 0, part], ref.at[1, 3], (after, up)),
                (me.at[0, 5, part], ref.at[1, 0], (after, down)),
                (me.at[3, 0, part], ref.at[0, 3], (before, up)),
                (me.at[3, 5, part], ref.at[0, 0], (before, down)),
            )
        ):
            mh.append(remote(src, dst, mh_s.at[k, i], mh_r.at[k, i], to))
    for c in mh:
        c.start()

    def to_plane(src, dst, s, r):
        def one(k, carry):
            e = lax.rem(d + k, D)
            remote(src(e), dst, s, r, (e, z)).start()
            return carry

        lax.fori_loop(1, D, one, 0)

    def from_plane(whole, s, r, both=True):
        rest = whole.at[pl.ds(0, D - 1)]
        c = remote(rest, rest, s, r, (after, z))
        c.wait_recv()
        c.wait_send()

    def to_chips(src, dst, s, r):
        def one(k, carry):
            e = lax.rem(chip + k, D // 2)
            remote(src, dst, s, r, (2 * e + core, z)).start()
            return carry

        lax.fori_loop(1, D // 2, one, 0)

    def from_chips(whole, s, r):
        rest = whole.at[pl.ds(0, D // 2 - 1), 0]
        remote(rest, rest, s, r, (sibling, z)).wait()

    to_chips(xc_ref, xg.at[chip, core], x_s, x_r)

    ch = []
    for ai, to_d in ((0, after), (1, d), (2, before)):
        for ud, to_z in ((0, up), (1, down)):
            for k, ref in ((0, xc_ref), (1, gc_ref)):
                i = (ai * 2 + ud) * 2 + k
                ch.append(
                    remote(
                        ref.at[pl.ds(64 * (1 - ud), 64)],
                        hr.at[ai, ud, k],
                        ch_s.at[i],
                        ch_r.at[i],
                        (to_d, to_z),
                    )
                )
    ch.append(remote(gc_ref, gd.at[0], ch_s.at[12], ch_r.at[12], (after, z)))
    ch.append(remote(gc_ref, gd.at[1], ch_s.at[13], ch_r.at[13], (before, z)))
    for c in ch:
        c.start()

    local[0].wait()
    for c in ga:
        c.wait()
    keep = pltpu.make_async_copy(ggl.at[d], gg.at[d], loc.at[4])
    keep.start()
    to_plane(lambda e: ggl.at[e], gg.at[d], gb_s, gb_r)

    local[3].wait()
    local[4].wait()
    for c in mh:
        c.wait()
    depth_ok = (d > 0, None, None, d < D - 1)
    height_ok = (z > 0, None, None, None, None, z < Z - 1)
    lane = lax.broadcasted_iota(jnp.int32, (64, 128), 1)
    for dd in range(4):
        for hh in range(6):
            row = me[dd, hh].astype(F32)
            for ok in (depth_ok[dd], height_ok[hh]):
                if ok is not None:
                    row = jnp.where(ok, row, 0.0)
            left = jnp.where(lane == 0, 0.0, pltpu.roll(row, 1, 1))
            right = jnp.where(lane == 127, 0.0, pltpu.roll(row, 127, 1))
            for c, v in enumerate((left, row, right)):
                v = v.astype(BF16)
                mv[dd, hh, 0, 32 * c : 32 * c + 32] = v[:32]
                mv[dd, hh, 1, 32 * c : 32 * c + 32] = v[32:]

    def columns(dd, k):
        return jnp.concatenate(
            [
                jnp.concatenate([mv[dd, h + b, k] for h in range(4)], axis=1)
                for b in range(3)
            ],
            axis=0,
        )

    seen = [
        jnp.concatenate([mv[dd + 1, h + 1, 1, 32:64] for h in range(4)], axis=1)
        for dd in range(2)
    ]
    grad = [None] * 3
    outs = [None] * 2
    for dd in range(4):
        cols = columns(dd, 0)
        part = dot(forward, cols, NN)
        for a in range(3):
            at = dd - a
            if 0 <= at < 2:
                p = part[32 * a : 32 * a + 32]
                outs[at] = p if outs[at] is None else outs[at] + p
                g = dot(seen[at], cols, NT)
                grad[a] = g if grad[a] is None else grad[a] + g
    flat = jnp.concatenate(grad + [jnp.zeros((32, 32), F32)], axis=1)
    for ob in range(4):
        for j in range(7):
            mr[ob * 7 + j] = flat[8 * ob : 8 * ob + 8, 128 * j : 128 * j + 128]
    for t in range(28, 32):
        mr[t] = jnp.zeros((8, 128), F32)
    keep_mr = pltpu.make_async_copy(mr.at[pl.ds(d * n, n)], mrl.at[d], loc.at[5])
    keep_mr.start()
    to_plane(lambda e: mr.at[pl.ds(e * n, n)], mrl.at[d], mr_s, mr_r)
    for at in range(2):
        for h in range(4):
            mo_ref[at, h] = outs[at][:, 128 * h : 128 * h + 128].astype(BF16)
    local[1].wait()
    from_chips(xg, x_s, x_r)
    x_on = remote(xg.at[:, core], xg.at[:, core], xf_s, xf_r, (sibling, z))
    x_on.start()
    to_chips(ws_ref, wg.at[chip, core], w_s, w_r)
    far = Z // 4
    last = (far, far - 1)
    half = zl.shape[1] // 2

    def hop(way, step, q):
        slot = lax.rem(pair + (step if way else Z // 2 - step), Z // 2)
        rows = zl.at[slot, pl.ds(half * q, half)]
        to = down_two if way else up_two
        return remote(
            rows, rows, ring_s.at[way, q, step], ring_r.at[way, q, step], (d, to)
        )

    def serve(step):
        for q in range(2):
            for way in range(2):
                if 0 < step <= last[way]:
                    hop(way, step - 1, q).wait_recv()
                if step < last[way]:
                    hop(way, step, q).start()

    def turn(way, hops, step):
        slot = lax.rem(z + (2 * step if way else Z - 2 * step), Z)
        rows = zm.at[slot]
        to = ((up, down), (up_two, down_two))[hops - 1][way]
        return remote(
            rows, rows, turn_s.at[way, hops - 1, step], turn_r.at[way, hops - 1, step], (d, to)
        )

    def turns(step):
        return [
            (way, hops, step)
            for way in range(2)
            for hops in (2, 1)
            if 0 <= step < far and 2 * step + hops <= Z // 2 - way
        ]

    def serve_middle(step):
        for t in turns(step - 1):
            if t[1] == 2:
                turn(*t).wait_recv()
        for t in turns(step):
            turn(*t).start()
        if step == far:
            for k in range(far):
                for t in turns(k):
                    if t[1] == 1:
                        turn(*t).wait_recv()

    keep_mr.wait()
    from_plane(mrl, mr_s, mr_r)
    total = mrl[0]
    for e in range(1, D):
        total = total + mrl[e]
    zm[z] = total.reshape(8 * n, 128)
    served = []
    last_gather = pltpu.make_async_copy(own, mg.at[d], loc.at[6])

    def advance():
        step = len(served)
        if step > far:
            return
        served.append(step)
        serve_middle(step)
        if step == far:
            whole = zm[0]
            for s in range(1, Z):
                whole = whole + zm[s]
            own[...] = (whole * middle_scale).reshape(n, 8, 128)
            last_gather.start()
            to_plane(lambda e: own, mg.at[d], mg_s, mg_r)

    advance()
    outs = [None] * 2
    for dd in range(4):
        part = dot(backward, columns(dd, 1), NN)
        for a in range(3):
            at = dd - a
            if 0 <= at < 2:
                p = part[32 * a : 32 * a + 32]
                outs[at] = p if outs[at] is None else outs[at] + p
    for at in range(2):
        for h in range(4):
            mdx_ref[at, h] = outs[at][:, 128 * h : 128 * h + 128].astype(BF16)

    advance()

    tf[...] = jnp.zeros(tf.shape, F32)
    keep.wait()
    from_plane(gg, gb_s, gb_r)
    lanes = lax.broadcasted_iota(jnp.int32, (D, CO, 128), 2)
    first = lanes < 64
    below = jnp.where(z > 0, gg[:, 0].astype(F32), 0.0)
    here = gg[:, 1].astype(F32)
    above = jnp.where(z < Z - 1, gg[:, 2].astype(F32), 0.0)

    def turned(v, amount):
        return pltpu.roll(v.reshape(D * CO, 128), amount, 1).reshape(D, CO, 128)

    here_half = turned(here, 64)
    bases = (
        jnp.where(first, here_half, turned(above, 64)),
        here,
        jnp.where(first, turned(below, 64), here_half),
    )
    column = lanes % 64
    for b in range(3):
        base = bases[b]
        shifted = (
            jnp.where(column == 63, 0.0, turned(base, 127)),
            base,
            jnp.where(column == 0, 0.0, turned(base, 1)),
        )
        for c in range(3):
            at = (b * 3 + c) * CO
            tf[1 : D + 1, at : at + CO, :] = shifted[c]
    advance()
    x_on.wait()

    def plane_pair(k, acc):
        s = 2 * k
        taps = jnp.concatenate(
            [
                tf[pl.ds(s, 3)].reshape(3 * RB, 128).astype(BF16),
                tf[pl.ds(s + 1, 3)].reshape(3 * RB, 128).astype(BF16),
            ],
            axis=1,
        )
        return acc + dot(taps, xg[k].reshape(256, 128), NN)

    acc = lax.fori_loop(0, D // 2, plane_pair, jnp.zeros((3 * RB, 128), F32))
    rows = [acc[(2 - a) * RB : (3 - a) * RB] for a in range(3)]
    spare = 2 * za.shape[1] - 3 * RB
    if spare:
        rows.append(jnp.zeros((spare, 128), F32))
    za[...] = jnp.concatenate(rows, axis=0).reshape(za.shape)
    share = remote(za.at[1 - side], zp, pair_s.at[0], pair_r.at[0], (d, other))
    share.start()
    advance()

    for c in ch:
        c.wait()
    row_ok = (z > 0, None, z < Z - 1)
    place = lax.broadcasted_iota(jnp.int32, (256, 128), 0) % 64
    for a in range(3):
        near = jnp.clip(d + a - 1, 0, D - 1)
        for k, col in ((0, xcol), (1, gcol)):
            if k == 0:
                centre = xg[near // 2, lax.rem(near, 2)]
            else:
                centre = gc_ref[...] if a == 1 else gd[a // 2]
            low = jnp.where(z > 0, hr[a, 0, k].astype(F32), 0.0)
            high = jnp.where(z < Z - 1, hr[a, 1, k].astype(F32), 0.0)
            rows = jnp.concatenate([low, centre.astype(F32), high], axis=0)
            if a == 0:
                rows = jnp.where(d > 0, rows, 0.0)
            if a == 2:
                rows = jnp.where(d < D - 1, rows, 0.0)
            prev = jnp.where(place == 0, 0.0, pltpu.roll(rows, 1, 0))
            nxt = jnp.where(place == 63, 0.0, pltpu.roll(rows, 255, 0))
            for c, v in enumerate((prev, rows, nxt)):
                col[a, :, 128 * c : 128 * c + 128] = v.astype(BF16)
    share.wait()
    zl[pair] = za[side] + zp[...]
    serve(0)
    advance()
    local[2].wait()
    from_chips(wg, w_s, w_r)
    w_on = remote(wg.at[:, core], wg.at[:, core], wf_s, wf_r, (sibling, z))
    w_on.start()
    for step in range(1, far + 1):
        serve(step)
        advance()

    total = zl[0]
    for s in range(1, Z // 2):
        total = total + zl[s]
    fin[side] = total * coarse_scale
    swap = remote(fin.at[side], fin.at[side], pair_s.at[1], pair_r.at[1], (d, other))
    swap.start()
    w_on.wait()

    def tap(t):
        w = wg[:, :, t].astype(F32)
        if CO % 8:
            w = jnp.concatenate([w[:, 0], w[:, 1]], axis=1)
        return w.reshape(128, 128).astype(BF16)

    out = jnp.zeros((128, 128), F32)
    dx = jnp.zeros((128, 128), F32)
    for a in range(3):
        for b in range(3):
            w = [tap((a * 3 + b) * 3 + c) for c in range(3)]
            out = out + dot(xcol[a, 64 * b : 64 * b + 128, :], jnp.concatenate(w, axis=1), NT)
            dx = dx + dot(
                gcol[2 - a, 64 * (2 - b) : 64 * (2 - b) + 128, :],
                jnp.concatenate(w[::-1], axis=0),
                NN,
            )
    co_ref[...] = out.astype(BF16)
    cdx_ref[...] = dx.astype(BF16)
    swap.wait()
    cw_ref[...] = fin[...].reshape(2 * fin.shape[1], 128)[: 3 * RB].reshape(3, RB, 128)
    for step in range(far):
        for q in range(2):
            for way in range(2):
                if step < last[way]:
                    hop(way, step, q).wait_send()
        for t in turns(step):
            turn(*t).wait_send()
    last_gather.wait()
    from_plane(mg, mg_s, mg_r)
    mw_ref[...] = mg[...]


def per_device(D, Z, middle_input, middle_cotangent, middle_weight, coarse_input, coarse_cotangent, coarse_weight):
    CO = 128 // D
    RB = -(-9 * CO // 8) * 8
    n = 32 // D
    H = -(-3 * RB // 16) * 8
    far = Z // 4
    middle_cells = middle_input.shape[0] * D * middle_input.shape[2] * Z * middle_input.shape[3]
    coarse_cells = coarse_input.shape[0] * D * coarse_input.shape[1] * Z * coarse_input.shape[2]
    mi = jnp.swapaxes(middle_input, 1, 2)
    mc = jnp.swapaxes(middle_cotangent, 1, 2)
    mk = middle_weight.reshape(27, 32, 32)
    xc = coarse_input.reshape(128, 128)
    gc = coarse_cotangent.reshape(128, 128)
    gt = gc.T.reshape(D, CO, 128)
    ws = jnp.swapaxes(coarse_weight, 3, 4).reshape(27, CO, 128)
    dma = pltpu.SemaphoreType.DMA
    vmem = pl.BlockSpec(memory_space=pltpu.VMEM)
    mo, mdx, mw, co, cdx, cw = pl.pallas_call(
        functools.partial(
            kernel, D, Z, 1.0 / math.sqrt(middle_cells), 1.0 / math.sqrt(coarse_cells)
        ),
        out_shape=(
            jax.ShapeDtypeStruct((2, 4, 32, 128), BF16),
            jax.ShapeDtypeStruct((2, 4, 32, 128), BF16),
            jax.ShapeDtypeStruct((D, n, 8, 128), F32),
            jax.ShapeDtypeStruct((128, 128), BF16),
            jax.ShapeDtypeStruct((128, 128), BF16),
            jax.ShapeDtypeStruct((3, RB, 128), F32),
        ),
        in_specs=[vmem] * 7,
        out_specs=(vmem,) * 6,
        scratch_shapes=[
            pltpu.VMEM((4, 6, 64, 128), BF16),
            pltpu.VMEM((4, 6, 2, 96, 128), BF16),
            pltpu.VMEM((32, 8, 128), F32),
            pltpu.VMEM((D, n, 8, 128), F32),
            pltpu.VMEM((n, 8, 128), F32),
            pltpu.VMEM((D // 2, 2, 128, 128), BF16),
            pltpu.VMEM((D // 2, 2, 27, CO, 128), BF16),
            pltpu.VMEM((D, 3, CO, 128), BF16),
            pltpu.VMEM((D, 3, CO, 128), BF16),
            pltpu.VMEM((D + 2, RB, 128), F32),
            pltpu.VMEM((3, 2, 2, 64, 128), BF16),
            pltpu.VMEM((2, 128, 128), BF16),
            pltpu.VMEM((3, 256, 384), BF16),
            pltpu.VMEM((3, 256, 384), BF16),
            pltpu.VMEM((2, H, 128), F32),
            pltpu.VMEM((H, 128), F32),
            pltpu.VMEM((Z // 2, H, 128), F32),
            pltpu.VMEM((2, H, 128), F32),
            pltpu.VMEM((Z, 8 * n, 128), F32),
            pltpu.VMEM((D, n, 8, 128), F32),
            dma((8,)),
            dma((2,)),
            dma((2,)),
            dma,
            dma,
            dma,
            dma,
            dma,
            dma,
            dma,
            dma,
            dma,
            dma,
            dma((14,)),
            dma((14,)),
            dma((2, 8)),
            dma((2, 8)),
            dma,
            dma,
            dma,
            dma,
            dma((2, 2, far)),
            dma((2, 2, far)),
            dma((2, 2, far)),
            dma((2, 2, far)),
            dma((2,)),
            dma((2,)),
        ],
        compiler_params=pltpu.CompilerParams(collective_id=0, has_side_effects=True),
    )(mi, mc, mk, xc, gc, gt, ws)
    middle_out = jnp.swapaxes(mo, 1, 2)
    middle_dx = jnp.swapaxes(mdx, 1, 2)
    tiles = mw.reshape(32, 8, 128)[:28].reshape(4, 7, 8, 128)
    flat = jnp.transpose(tiles, (0, 2, 1, 3)).reshape(32, 896)[:, :864]
    middle_dw = flat.T.reshape(3, 3, 3, 32, 32)
    coarse_dw = jnp.swapaxes(cw[:, : 9 * CO].reshape(3, 3, 3, CO, 128), 3, 4)
    return (
        middle_out,
        middle_dx,
        middle_dw,
        co.reshape(coarse_input.shape),
        cdx.reshape(coarse_input.shape),
        coarse_dw,
    )


def solution(mesh):
    placed = (
        P("depth", None, "height", None),
        P("depth", None, "height", None),
        P(),
        P("depth", "height", None, None),
        P("depth", "height", None, None),
        P(None, None, None, None, "depth"),
    )
    return jax.shard_map(
        functools.partial(per_device, mesh.shape["depth"], mesh.shape["height"]),
        mesh=mesh,
        in_specs=placed,
        out_specs=(
            placed[0],
            placed[1],
            P(),
            placed[3],
            placed[4],
            placed[5],
        ),
        check_vma=False,
    )
```

```python
import functools
import math

import jax
import jax.numpy as jnp
from jax import lax
from jax.experimental import pallas as pl
from jax.experimental.pallas import tpu as pltpu
from jax.sharding import PartitionSpec as P

MESH = pl.DeviceIdType.MESH
F32 = jnp.float32
BF16 = jnp.bfloat16
NT = (((1,), (1,)), ((), ()))
NN = (((1,), (0,)), ((), ()))


def dot(a, b, dims):
    return lax.dot_general(a, b, dims, preferred_element_type=F32)


def kernel(
    D,
    Z,
    middle_scale,
    coarse_scale,
    mi_ref,
    mc_ref,
    mk_ref,
    xc_ref,
    gc_ref,
    gt_ref,
    ws_ref,
    mo_ref,
    mw_ref,
    co_ref,
    cw_ref,
    me,
    mv,
    mr,
    mrl,
    own,
    xg,
    wg,
    ggl,
    gg,
    tf,
    hr,
    gd,
    xcol,
    gcol,
    za,
    zp,
    zl,
    fin,
    zm,
    mg,
    loc,
    ga_s,
    ga_r,
    x_s,
    x_r,
    xf_s,
    xf_r,
    gb_s,
    gb_r,
    w_s,
    w_r,
    wf_s,
    wf_r,
    ch_s,
    ch_r,
    mh_s,
    mh_r,
    mr_s,
    mr_r,
    mg_s,
    mg_r,
    ring_s,
    ring_r,
    turn_s,
    turn_r,
    pair_s,
    pair_r,
):
    d = lax.axis_index("depth")
    z = lax.axis_index("height")
    CO = 128 // D
    RB = tf.shape[1]
    n = 32 // D
    chip = d // 2
    core = lax.rem(d, 2)
    sibling = 2 * chip + 1 - core
    up = lax.rem(z + 1, Z)
    down = lax.rem(z + Z - 1, Z)
    after = lax.rem(d + 1, D)
    before = lax.rem(d + D - 1, D)
    up_two = lax.rem(z + 2, Z)
    down_two = lax.rem(z + Z - 2, Z)
    pair = z // 2
    side = lax.rem(z, 2)
    other = z + 1 - 2 * side

    barrier = pltpu.get_barrier_semaphore()

    def greet(k, carry):
        pl.semaphore_signal(
            barrier, inc=1, device_id=(lax.rem(d + k, D), z), device_id_type=MESH
        )
        return carry

    for zz in (up, down):
        for dd in (before, d, after):
            pl.semaphore_signal(barrier, inc=1, device_id=(dd, zz), device_id_type=MESH)
    for zz in (up_two, down_two):
        pl.semaphore_signal(barrier, inc=1, device_id=(d, zz), device_id_type=MESH)
    lax.fori_loop(1, D, greet, 0)

    taps = [mk_ref[t].astype(F32) for t in range(27)]
    forward = jnp.concatenate(
        [
            jnp.concatenate([taps[9 * a + t].T for t in range(9)], axis=1)
            for a in range(3)
        ],
        axis=0,
    ).astype(BF16)
    backward = jnp.concatenate(
        [
            jnp.concatenate([taps[26 - 9 * a - t] for t in range(9)], axis=1)
            for a in range(3)
        ],
        axis=0,
    ).astype(BF16)
    pl.semaphore_wait(barrier, D - 1 + 8)

    def remote(src, dst, s, r, to):
        return pltpu.make_async_remote_copy(
            src_ref=src, dst_ref=dst, send_sem=s, recv_sem=r, device_id=to, device_id_type=MESH
        )

    local = [
        pltpu.make_async_copy(gt_ref, ggl.at[:, 1], loc.at[0]),
        pltpu.make_async_copy(xc_ref, xg.at[chip, core], loc.at[1]),
        pltpu.make_async_copy(ws_ref, wg.at[chip, core], loc.at[2]),
        pltpu.make_async_copy(mi_ref, me.at[1:3, 1:5, 0:32], loc.at[3]),
        pltpu.make_async_copy(mc_ref, me.at[1:3, 1:5, 32:64], loc.at[7]),
    ]
    for c in local:
        c.start()

    ga = [
        remote(gt_ref, ggl.at[:, 0], ga_s.at[0], ga_r.at[0], (d, up)),
        remote(gt_ref, ggl.at[:, 2], ga_s.at[1], ga_r.at[1], (d, down)),
    ]
    for c in ga:
        c.start()

    mh = []
    for k, ref in ((0, mi_ref), (1, mc_ref)):
        part = slice(32 * k, 32 * k + 32)
        for i, (dst, src, to) in enumerate(
            (
                (me.at[0, 1:5, part], ref.at[1], (after, z)),
                (me.at[3, 1:5, part], ref.at[0], (before, z)),
                (me.at[1:3, 0, part], ref.at[:, 3], (d, up)),
                (me.at[1:3, 5, part], ref.at[:, 0], (d, down)),
                (me.at[0, 0, part], ref.at[1, 3], (after, up)),
                (me.at[0, 5, part], ref.at[1, 0], (after, down)),
                (me.at[3, 0, part], ref.at[0, 3], (before, up)),
                (me.at[3, 5, part], ref.at[0, 0], (before, down)),
            )
        ):
            mh.append(remote(src, dst, mh_s.at[k, i], mh_r.at[k, i], to))
    for c in mh:
        c.start()

    def to_plane(src, dst, s, r):
        def one(k, carry):
            e = lax.rem(d + k, D)
            remote(src(e), dst, s, r, (e, z)).start()
            return carry

        lax.fori_loop(1, D, one, 0)

    def from_plane(whole, s, r, both=True):
        rest = whole.at[pl.ds(0, D - 1)]
        c = remote(rest, rest, s, r, (after, z))
        c.wait_recv()
        c.wait_send()

    def to_chips(src, dst, s, r):
        def one(k, carry):
            e = lax.rem(chip + k, D // 2)
            remote(src, dst, s, r, (2 * e + core, z)).start()
            return carry

        lax.fori_loop(1, D // 2, one, 0)

    def from_chips(whole, s, r):
        rest = whole.at[pl.ds(0, D // 2 - 1), 0]
        remote(rest, rest, s, r, (sibling, z)).wait()

    to_chips(xc_ref, xg.at[chip, core], x_s, x_r)

    ch = []
    for ai, to_d in ((0, after), (1, d), (2, before)):
        for ud, to_z in ((0, up), (1, down)):
            for k, ref in ((0, xc_ref), (1, gc_ref)):
                i = (ai * 2 + ud) * 2 + k
                ch.append(
                    remote(
                        ref.at[pl.ds(64 * (1 - ud), 64)],
                        hr.at[ai, ud, k],
                        ch_s.at[i],
                        ch_r.at[i],
                        (to_d, to_z),
                    )
                )
    ch.append(remote(gc_ref, gd.at[0], ch_s.at[12], ch_r.at[12], (after, z)))
    ch.append(remote(gc_ref, gd.at[1], ch_s.at[13], ch_r.at[13], (before, z)))
    for c in ch:
        c.start()

    local[0].wait()
    for c in ga:
        c.wait()
    keep = pltpu.make_async_copy(ggl.at[d], gg.at[d], loc.at[4])
    keep.start()
    to_plane(lambda e: ggl.at[e], gg.at[d], gb_s, gb_r)

    local[3].wait()
    local[4].wait()
    for c in mh:
        c.wait()
    depth_ok = (d > 0, None, None, d < D - 1)
    height_ok = (z > 0, None, None, None, None, z < Z - 1)
    lane = lax.broadcasted_iota(jnp.int32, (64, 128), 1)
    for dd in range(4):
        for hh in range(6):
            row = me[dd, hh].astype(F32)
            for ok in (depth_ok[dd], height_ok[hh]):
                if ok is not None:
                    row = jnp.where(ok, row, 0.0)
            left = jnp.where(lane == 0, 0.0, pltpu.roll(row, 1, 1))
            right = jnp.where(lane == 127, 0.0, pltpu.roll(row, 127, 1))
            for c, v in enumerate((left, row, right)):
                v = v.astype(BF16)
                mv[dd, hh, 0, 32 * c : 32 * c + 32] = v[:32]
                mv[dd, hh, 1, 32 * c : 32 * c + 32] = v[32:]

    def columns(dd, k):
        return jnp.concatenate(
            [
                jnp.concatenate([mv[dd, h + b, k] for h in range(4)], axis=1)
                for b in range(3)
            ],
            axis=0,
        )

    seen = [
        jnp.concatenate([mv[dd + 1, h + 1, 1, 32:64] for h in range(4)], axis=1)
        for dd in range(2)
    ]
    grad = [None] * 3
    outs = [None] * 2
    for dd in range(4):
        cols = columns(dd, 0)
        part = dot(forward, cols, NN)
        for a in range(3):
            at = dd - a
            if 0 <= at < 2:
                p = part[32 * a : 32 * a + 32]
                outs[at] = p if outs[at] is None else outs[at] + p
                g = dot(seen[at], cols, NT)
                grad[a] = g if grad[a] is None else grad[a] + g
    flat = jnp.concatenate(grad + [jnp.zeros((32, 32), F32)], axis=1)
    for ob in range(4):
        for j in range(7):
            mr[ob * 7 + j] = flat[8 * ob : 8 * ob + 8, 128 * j : 128 * j + 128]
    for t in range(28, 32):
        mr[t] = jnp.zeros((8, 128), F32)
    keep_mr = pltpu.make_async_copy(mr.at[pl.ds(d * n, n)], mrl.at[d], loc.at[5])
    keep_mr.start()
    to_plane(lambda e: mr.at[pl.ds(e * n, n)], mrl.at[d], mr_s, mr_r)
    for at in range(2):
        for h in range(4):
            mo_ref[0, at, h] = outs[at][:, 128 * h : 128 * h + 128].astype(BF16)
    local[1].wait()
    from_chips(xg, x_s, x_r)
    x_on = remote(xg.at[:, core], xg.at[:, core], xf_s, xf_r, (sibling, z))
    x_on.start()
    to_chips(ws_ref, wg.at[chip, core], w_s, w_r)
    far = Z // 4
    last = (far, far - 1)
    half = zl.shape[1] // 2

    def hop(way, step, q):
        slot = lax.rem(pair + (step if way else Z // 2 - step), Z // 2)
        rows = zl.at[slot, pl.ds(half * q, half)]
        to = down_two if way else up_two
        return remote(
            rows, rows, ring_s.at[way, q, step], ring_r.at[way, q, step], (d, to)
        )

    def serve(step):
        for q in range(2):
            for way in range(2):
                if 0 < step <= last[way]:
                    hop(way, step - 1, q).wait_recv()
                if step < last[way]:
                    hop(way, step, q).start()

    def turn(way, hops, step):
        slot = lax.rem(z + (2 * step if way else Z - 2 * step), Z)
        rows = zm.at[slot]
        to = ((up, down), (up_two, down_two))[hops - 1][way]
        return remote(
            rows, rows, turn_s.at[way, hops - 1, step], turn_r.at[way, hops - 1, step], (d, to)
        )

    def turns(step):
        return [
            (way, hops, step)
            for way in range(2)
            for hops in (2, 1)
            if 0 <= step < far and 2 * step + hops <= Z // 2 - way
        ]

    def serve_middle(step):
        for t in turns(step - 1):
            if t[1] == 2:
                turn(*t).wait_recv()
        for t in turns(step):
            turn(*t).start()
        if step == far:
            for k in range(far):
                for t in turns(k):
                    if t[1] == 1:
                        turn(*t).wait_recv()

    keep_mr.wait()
    from_plane(mrl, mr_s, mr_r)
    total = mrl[0]
    for e in range(1, D):
        total = total + mrl[e]
    zm[z] = total.reshape(8 * n, 128)
    served = []
    last_gather = pltpu.make_async_copy(own, mg.at[d], loc.at[6])

    def advance():
        step = len(served)
        if step > far:
            return
        served.append(step)
        serve_middle(step)
        if step == far:
            whole = zm[0]
            for s in range(1, Z):
                whole = whole + zm[s]
            own[...] = (whole * middle_scale).reshape(n, 8, 128)
            last_gather.start()
            to_plane(lambda e: own, mg.at[d], mg_s, mg_r)

    advance()
    outs = [None] * 2
    for dd in range(4):
        part = dot(backward, columns(dd, 1), NN)
        for a in range(3):
            at = dd - a
            if 0 <= at < 2:
                p = part[32 * a : 32 * a + 32]
                outs[at] = p if outs[at] is None else outs[at] + p
    for at in range(2):
        for h in range(4):
            mo_ref[1, at, h] = outs[at][:, 128 * h : 128 * h + 128].astype(BF16)

    tf[...] = jnp.zeros(tf.shape, F32)
    keep.wait()
    from_plane(gg, gb_s, gb_r)
    lanes = lax.broadcasted_iota(jnp.int32, (D, CO, 128), 2)
    first = lanes < 64
    below = jnp.where(z > 0, gg[:, 0].astype(F32), 0.0)
    here = gg[:, 1].astype(F32)
    above = jnp.where(z < Z - 1, gg[:, 2].astype(F32), 0.0)

    def turned(v, amount):
        return pltpu.roll(v.reshape(D * CO, 128), amount, 1).reshape(D, CO, 128)

    here_half = turned(here, 64)
    bases = (
        jnp.where(first, here_half, turned(above, 64)),
        here,
        jnp.where(first, turned(below, 64), here_half),
    )
    column = lanes % 64
    for b in range(3):
        base = bases[b]
        shifted = (
            jnp.where(column == 63, 0.0, turned(base, 127)),
            base,
            jnp.where(column == 0, 0.0, turned(base, 1)),
        )
        for c in range(3):
            at = (b * 3 + c) * CO
            tf[1 : D + 1, at : at + CO, :] = shifted[c]
    x_on.wait()

    def plane_pair(k, acc):
        s = 2 * k
        taps = jnp.concatenate(
            [
                tf[pl.ds(s, 3)].reshape(3 * RB, 128).astype(BF16),
                tf[pl.ds(s + 1, 3)].reshape(3 * RB, 128).astype(BF16),
            ],
            axis=1,
        )
        return acc + dot(taps, xg[k].reshape(256, 128), NN)

    acc = lax.fori_loop(0, D // 2, plane_pair, jnp.zeros((3 * RB, 128), F32))
    rows = [acc[(2 - a) * RB : (3 - a) * RB] for a in range(3)]
    spare = 2 * za.shape[1] - 3 * RB
    if spare:
        rows.append(jnp.zeros((spare, 128), F32))
    za[...] = jnp.concatenate(rows, axis=0).reshape(za.shape)
    share = remote(za.at[1 - side], zp, pair_s.at[0], pair_r.at[0], (d, other))
    share.start()
    advance()

    for c in ch:
        c.wait()
    row_ok = (z > 0, None, z < Z - 1)
    place = lax.broadcasted_iota(jnp.int32, (256, 128), 0) % 64
    for a in range(3):
        near = jnp.clip(d + a - 1, 0, D - 1)
        for k, col in ((0, xcol), (1, gcol)):
            if k == 0:
                centre = xg[near // 2, lax.rem(near, 2)]
            else:
                centre = gc_ref[...] if a == 1 else gd[a // 2]
            low = jnp.where(z > 0, hr[a, 0, k].astype(F32), 0.0)
            high = jnp.where(z < Z - 1, hr[a, 1, k].astype(F32), 0.0)
            rows = jnp.concatenate([low, centre.astype(F32), high], axis=0)
            if a == 0:
                rows = jnp.where(d > 0, rows, 0.0)
            if a == 2:
                rows = jnp.where(d < D - 1, rows, 0.0)
            prev = jnp.where(place == 0, 0.0, pltpu.roll(rows, 1, 0))
            nxt = jnp.where(place == 63, 0.0, pltpu.roll(rows, 255, 0))
            for c, v in enumerate((prev, rows, nxt)):
                col[a, :, 128 * c : 128 * c + 128] = v.astype(BF16)
    share.wait()
    zl[pair] = za[side] + zp[...]
    serve(0)
    advance()
    local[2].wait()
    from_chips(wg, w_s, w_r)
    w_on = remote(wg.at[:, core], wg.at[:, core], wf_s, wf_r, (sibling, z))
    w_on.start()
    for step in range(1, far + 1):
        serve(step)
        advance()

    total = zl[0]
    for s in range(1, Z // 2):
        total = total + zl[s]
    fin[side] = total * coarse_scale
    swap = remote(fin.at[side], fin.at[side], pair_s.at[1], pair_r.at[1], (d, other))
    swap.start()
    w_on.wait()

    def tap(t):
        w = wg[:, :, t].astype(F32)
        if CO % 8:
            w = jnp.concatenate([w[:, 0], w[:, 1]], axis=1)
        return w.reshape(128, 128).astype(BF16)

    out = jnp.zeros((128, 128), F32)
    dx = jnp.zeros((128, 128), F32)
    for a in range(3):
        for b in range(3):
            w = [tap((a * 3 + b) * 3 + c) for c in range(3)]
            out = out + dot(xcol[a, 64 * b : 64 * b + 128, :], jnp.concatenate(w, axis=1), NT)
            dx = dx + dot(
                gcol[2 - a, 64 * (2 - b) : 64 * (2 - b) + 128, :],
                jnp.concatenate(w[::-1], axis=0),
                NN,
            )
    co_ref[0] = out.astype(BF16)
    co_ref[1] = dx.astype(BF16)
    swap.wait()
    cw_ref[...] = fin[...].reshape(2 * fin.shape[1], 128)[: 3 * RB].reshape(3, RB, 128)
    for step in range(far):
        for q in range(2):
            for way in range(2):
                if step < last[way]:
                    hop(way, step, q).wait_send()
        for t in turns(step):
            turn(*t).wait_send()
    last_gather.wait()
    from_plane(mg, mg_s, mg_r)
    mw_ref[...] = mg[...]


def per_device(D, Z, middle_input, middle_cotangent, middle_weight, coarse_input, coarse_cotangent, coarse_weight):
    CO = 128 // D
    RB = -(-9 * CO // 8) * 8
    n = 32 // D
    H = -(-3 * RB // 16) * 8
    far = Z // 4
    middle_cells = middle_input.shape[0] * D * middle_input.shape[2] * Z * middle_input.shape[3]
    coarse_cells = coarse_input.shape[0] * D * coarse_input.shape[1] * Z * coarse_input.shape[2]
    mi = jnp.swapaxes(middle_input, 1, 2)
    mc = jnp.swapaxes(middle_cotangent, 1, 2)
    mk = middle_weight.reshape(27, 32, 32)
    xc = coarse_input.reshape(128, 128)
    gc = coarse_cotangent.reshape(128, 128)
    gt = gc.T.reshape(D, CO, 128)
    ws = jnp.swapaxes(coarse_weight, 3, 4).reshape(27, CO, 128)
    dma = pltpu.SemaphoreType.DMA
    vmem = pl.BlockSpec(memory_space=pltpu.VMEM)
    mo, mw, co, cw = pl.pallas_call(
        functools.partial(
            kernel, D, Z, 1.0 / math.sqrt(middle_cells), 1.0 / math.sqrt(coarse_cells)
        ),
        out_shape=(
            jax.ShapeDtypeStruct((2, 2, 4, 32, 128), BF16),
            jax.ShapeDtypeStruct((D, n, 8, 128), F32),
            jax.ShapeDtypeStruct((2, 128, 128), BF16),
            jax.ShapeDtypeStruct((3, RB, 128), F32),
        ),
        in_specs=[vmem] * 7,
        out_specs=(vmem,) * 4,
        scratch_shapes=[
            pltpu.VMEM((4, 6, 64, 128), BF16),
            pltpu.VMEM((4, 6, 2, 96, 128), BF16),
            pltpu.VMEM((32, 8, 128), F32),
            pltpu.VMEM((D, n, 8, 128), F32),
            pltpu.VMEM((n, 8, 128), F32),
            pltpu.VMEM((D // 2, 2, 128, 128), BF16),
            pltpu.VMEM((D // 2, 2, 27, CO, 128), BF16),
            pltpu.VMEM((D, 3, CO, 128), BF16),
            pltpu.VMEM((D, 3, CO, 128), BF16),
            pltpu.VMEM((D + 2, RB, 128), F32),
            pltpu.VMEM((3, 2, 2, 64, 128), BF16),
            pltpu.VMEM((2, 128, 128), BF16),
            pltpu.VMEM((3, 256, 384), BF16),
            pltpu.VMEM((3, 256, 384), BF16),
            pltpu.VMEM((2, H, 128), F32),
            pltpu.VMEM((H, 128), F32),
            pltpu.VMEM((Z // 2, H, 128), F32),
            pltpu.VMEM((2, H, 128), F32),
            pltpu.VMEM((Z, 8 * n, 128), F32),
            pltpu.VMEM((D, n, 8, 128), F32),
            dma((8,)),
            dma((2,)),
            dma((2,)),
            dma,
            dma,
            dma,
            dma,
            dma,
            dma,
            dma,
            dma,
            dma,
            dma,
            dma((14,)),
            dma((14,)),
            dma((2, 8)),
            dma((2, 8)),
            dma,
            dma,
            dma,
            dma,
            dma((2, 2, far)),
            dma((2, 2, far)),
            dma((2, 2, far)),
            dma((2, 2, far)),
            dma((2,)),
            dma((2,)),
        ],
        compiler_params=pltpu.CompilerParams(collective_id=0, has_side_effects=True),
    )(mi, mc, mk, xc, gc, gt, ws)
    middle_out = jnp.swapaxes(mo[0], 1, 2)
    middle_dx = jnp.swapaxes(mo[1], 1, 2)
    tiles = mw.reshape(32, 8, 128)[:28].reshape(4, 7, 8, 128)
    flat = jnp.transpose(tiles, (0, 2, 1, 3)).reshape(32, 896)[:, :864]
    middle_dw = flat.T.reshape(3, 3, 3, 32, 32)
    coarse_dw = jnp.swapaxes(cw[:, : 9 * CO].reshape(3, 3, 3, CO, 128), 3, 4)
    return (
        middle_out,
        middle_dx,
        middle_dw,
        co[0].reshape(coarse_input.shape),
        co[1].reshape(coarse_input.shape),
        coarse_dw,
    )


def solution(mesh):
    placed = (
        P("depth", None, "height", None),
        P("depth", None, "height", None),
        P(),
        P("depth", "height", None, None),
        P("depth", "height", None, None),
        P(None, None, None, None, "depth"),
    )
    return jax.shard_map(
        functools.partial(per_device, mesh.shape["depth"], mesh.shape["height"]),
        mesh=mesh,
        in_specs=placed,
        out_specs=(
            placed[0],
            placed[1],
            P(),
            placed[3],
            placed[4],
            placed[5],
        ),
        check_vma=False,
    )
```
